256 devices in a mesh: bead: 32 (over x, y, core), wave: 4 (over z_hi), grp: 2 (over z_lo).
Axes of the slice: x: 4, y: 4, z: 8 (z_hi: 4, z_lo: 2; z = z_hi * 2 + z_lo), core: 2. Of those that a mesh axis runs over, the one named last changes fastest.
Arguments:
- features: float32 [32768, 512], P(('bead', 'wave', 'grp')), may hold values from -6 to 6
- positions: float32 [3, 32768], P(None, ('bead', 'wave', 'grp')), may hold values from 0 to 1
- wavevectors: int32 [3, 4096], P(None, ('wave', 'grp')), may hold values from -6 to 6
- neighbour_slots: int32 [32, 32768], P(None, ('bead', 'wave', 'grp')), may hold values from 0 to 383
- neighbour_count: int32 [32768], P(('bead', 'wave', 'grp')), may hold values from 8 to 32
- pair_distance: float32 [32, 32768], P(None, ('bead', 'wave', 'grp')), may hold values from 0.3 to 2.4
- w_self: float32 [512, 512], replicated, may hold values from -0.25 to 0.25
- w_neighbour: float32 [512, 512], replicated, may hold values from -0.25 to 0.25
- w_edge: float32 [16, 512], replicated, may hold values from -1.5 to 1.5
- w_message: float32 [512, 512], replicated, may hold values from -0.25 to 0.25
- spec_filter: float32 [4096, 512], P(('wave', 'grp')), may hold values from -4 to 4
- norm_gain: float32 [512], replicated, may hold values from 0.5 to 1.5
- w_up: float32 [512, 512], replicated, may hold values from -0.25 to 0.25
- w_down: float32 [512, 512], replicated, may hold values from -0.25 to 0.25
Outputs:
- updated: float32 [32768, 512], P(('bead', 'wave', 'grp'))
The draws below stay inside these ranges and needn't reach their ends.
All inputs are finite; a program needn't handle non-finite values.
Results may differ from the reference program's by a relative error of at most 0.0003.
Values sent between devices are 32-bit elements; how exact they have to be, the bound alone decides.
No kernel may reach another device: no remote copies, remote signals or barrier semaphores. Data moves between devices by JAX's collectives and lax.ppermute only.
A program may use at most 128 MiB of HBM per device.

```python
import jax
import jax.numpy as jnp
from jax import lax

D = 512
KVEC = 4096
RBF = 16
KNB = 32
BLOCK = 128
BEADS = 32768


def place_ends(drawn, rng, smallest, top_value):
    index_at = [jax.random.randint(jax.random.fold_in(rng, axis), (), 0, length) for axis, length in enumerate(drawn.shape)]
    main_axis = drawn.shape.index(max(drawn.shape))
    beside = index_at[:main_axis] + [(index_at[main_axis] + 1) % drawn.shape[main_axis]] + index_at[main_axis + 1:]
    return drawn.at[tuple(index_at)].set(smallest).at[tuple(beside)].set(top_value)


def steps_of(own_key, extent, shards, low, high):
    loudness = 1.0
    for position, blocks in shards:
        heights = jax.random.uniform(jax.random.fold_in(jax.random.fold_in(own_key, 6), position), (blocks,), jnp.float32, low / len(shards), high / len(shards))
        loudness = loudness * jnp.repeat(jnp.exp(heights), extent[position] // blocks).reshape((-1,) + (1,) * (len(extent) - 1 - position))
    return loudness


def bell_draw(key, dims, scale, most, split=(), held_as=jnp.bfloat16):
    values = jax.random.normal(key, dims, jnp.float32) * scale
    if len(split) > 0:
        values = steps_of(key, dims, split, -0.22, 0.18) * values
    return jnp.clip(values, min=-most, max=most).astype(held_as)


def setup_inputs(seed: int = 0) -> dict:
    key_list = jax.random.split(jax.random.key(seed), 15)
    features = bell_draw(key_list[0], (BEADS, D), 1.0, 6.0, ((0, 256),), jnp.float32)
    positions = jnp.clip(1.0 * jax.random.uniform(key_list[1], (3, BEADS), jnp.float32) ** steps_of(key_list[1], (3, BEADS), ((1, 256),), -0.2, 0.2), 0.0, 1.0)
    wavevectors = place_ends(jax.random.randint(key_list[2], (3, KVEC), -6, 7), jax.random.fold_in(key_list[2], 1), -6, 6).astype(jnp.int32)
    neighbour_slots = place_ends(jax.random.randint(key_list[3], (KNB, BEADS), 0, 3 * BLOCK), jax.random.fold_in(key_list[3], 1), 0, (3 * BLOCK) - 1).astype(jnp.int32)
    neighbour_count = place_ends(jax.random.randint(key_list[4], (BEADS,), KNB // 4, KNB + 1), jax.random.fold_in(key_list[4], 1), KNB // 4, KNB).astype(jnp.int32)
    pair_distance = jnp.clip(0.3 + 2.1000001 * jax.random.uniform(key_list[5], (KNB, BEADS), jnp.float32) ** steps_of(key_list[5], (KNB, BEADS), ((1, 256),), -0.2, 0.2), 0.3, 2.4)
    w_self = bell_draw(key_list[6], (D, D), D ** -0.5, 0.25, (), jnp.float32)
    w_neighbour = bell_draw(key_list[7], (D, D), D ** -0.5, 0.25, (), jnp.float32)
    w_edge = bell_draw(key_list[8], (RBF, D), RBF ** -0.5, 1.5, (), jnp.float32)
    w_message = bell_draw(key_list[9], (D, D), D ** -0.5, 0.25, (), jnp.float32)
    spec_filter = bell_draw(key_list[10], (KVEC, D), 1.0, 4.0, ((0, 8),), jnp.float32)
    norm_gain = jnp.clip(1.0 + 0.1 * jax.random.normal(key_list[11], (D,), jnp.float32), 0.5, 1.5)
    w_up = bell_draw(key_list[12], (D, D), D ** -0.5, 0.25, (), jnp.float32)
    w_down = bell_draw(key_list[13], (D, D), D ** -0.5, 0.25, (), jnp.float32)
    return dict(features=features, positions=positions, wavevectors=wavevectors, neighbour_slots=neighbour_slots, neighbour_count=neighbour_count, pair_distance=pair_distance, w_self=w_self, w_neighbour=w_neighbour, w_edge=w_edge, w_message=w_message, spec_filter=spec_filter, norm_gain=norm_gain, w_up=w_up, w_down=w_down)


highest = lax.Precision.HIGHEST
epsilon = 1e-05
reach = 2.5
two_pi = 6.283185307179586

def matmul(left, right):
    return jnp.dot(left, right, precision=highest, preferred_element_type=jnp.float32)

def short_rows(self_proj, window, slot_index, count, distance, w_edge, w_message):
    slots, rows = slot_index.shape
    width = window.shape[1]
    picked = jnp.take(window, slot_index.reshape(-1), axis=0).reshape(slots, rows, width)
    radial = w_edge.shape[0]
    spacing = reach / (radial - 1)
    centers = jnp.arange(radial, dtype=jnp.float32) * spacing
    basis = jnp.exp(-jnp.square((distance[:, :, None] - centers) / spacing))
    edge = matmul(basis.reshape(slots * rows, radial), w_edge).reshape(slots, rows, width)
    message = jax.nn.silu(self_proj[None] + picked + edge)
    valid = (jnp.arange(slots, dtype=jnp.int32)[:, None] < count[None, :]).astype(jnp.float32)
    summed = lax.optimization_barrier(jnp.sum(message * valid[:, :, None], axis=0)) / slots
    return matmul(summed, w_message)

def phase_table(coords, vectors):
    angle = coords[0][:, None] * vectors[0][None, :] + coords[1][:, None] * vectors[1][None, :]
    angle = angle + coords[2][:, None] * vectors[2][None, :]
    angle = two_pi * angle
    return (jnp.cos(angle), jnp.sin(angle))

def reference(features, positions, wavevectors, neighbour_slots, neighbour_count, pair_distance, w_self, w_neighbour, w_edge, w_message, spec_filter, norm_gain, w_up, w_down):
    beads, width = features.shape
    nblocks = beads // BLOCK
    self_proj = matmul(features, w_self)
    neighbour_proj = matmul(features, w_neighbour)
    padded = jnp.pad(neighbour_proj, ((BLOCK, BLOCK), (0, 0)))

    def one_block(block):
        start = (block * BLOCK).astype(jnp.int32)
        own = lax.dynamic_slice_in_dim(self_proj, start, BLOCK, 0)
        window = lax.dynamic_slice_in_dim(padded, start, 3 * BLOCK, 0)
        slot_index = lax.dynamic_slice_in_dim(neighbour_slots, start, BLOCK, 1)
        count = lax.dynamic_slice_in_dim(neighbour_count, start, BLOCK, 0)
        distance = lax.dynamic_slice_in_dim(pair_distance, start, BLOCK, 1)
        return short_rows(own, window, slot_index, count, distance, w_edge, w_message)
    short = lax.map(one_block, jnp.arange(nblocks, dtype=jnp.int32)).reshape(beads, width)
    kblock = min(KVEC, 512)
    nk = KVEC // kblock
    vec_blocks = wavevectors.astype(jnp.float32).reshape(3, nk, kblock).transpose(1, 0, 2)

    def forward(vectors):
        cosine, sine = phase_table(positions, vectors)
        cos_part = jnp.einsum('nk,nd->kd', cosine, features, precision=highest)
        sin_part = jnp.einsum('nk,nd->kd', sine, features, precision=highest)
        return (cos_part, sin_part)
    cos_factor, sin_factor = lax.map(forward, vec_blocks)
    power = lax.optimization_barrier(jnp.sum(jnp.square(cos_factor) + jnp.square(sin_factor), axis=(0, 1)))
    scale = lax.rsqrt(power / (2 * KVEC) + epsilon)
    filt_blocks = spec_filter.reshape(nk, kblock, width)
    filt_cos = filt_blocks * cos_factor * scale
    filt_sin = filt_blocks * sin_factor * scale

    def inverse(carry, item):
        vectors, fc, fs = item
        cosine, sine = phase_table(positions, vectors)
        return (carry + matmul(cosine, fc) + matmul(sine, fs), None)
    long_sum, unused = lax.scan(inverse, jnp.zeros((beads, width), jnp.float32), (vec_blocks, filt_cos, filt_sin))
    long_range = long_sum / jnp.sqrt(jnp.float32(KVEC))
    total = features + short + long_range
    normed = total * lax.rsqrt(lax.optimization_barrier(jnp.mean(jnp.square(total), axis=1, keepdims=True)) + epsilon) * norm_gain
    return total + matmul(jax.nn.silu(matmul(normed, w_up)), w_down)
```

```python
import functools

import jax
import jax.numpy as jnp
from jax import lax
from jax.experimental import pallas as pl
from jax.experimental.pallas import tpu as pltpu
from jax.sharding import Mesh, PartitionSpec as P

KVEC = 4096
BLOCK = 128
WIDTH = 512
SLOTS = 32
RADIAL = 16
epsilon = 1e-05
reach = 2.5

TRADE = ("core", "zh", "zl")
TOTAL = ("x", "y")
EVERY = ("x", "y", "core", "zh", "zl")
FEATS = 32
AT_POS = 32
AT_VEC = 35
AT_FILTER = 41
ROWS = 48
USED = tuple(range(7)) + tuple(range(9, 15))

SIN = (6.283182792843448, -41.3414193330158, 81.59613740878913, -76.57967400034956,
       41.20368207513971, -12.268761447381701)
COS = (0.9999999890563522, -19.73920449855691, 64.93911741205494, -85.45013861232991,
       60.16762307755092, -25.967568454487537, 6.528613369793176)

bf16 = jnp.bfloat16
f32 = jnp.float32
NT = (((1,), (1,)), ((), ()))


def halves(value):
    high = value.astype(bf16)
    return high, (value - high.astype(f32)).astype(bf16)


def dot(left, right):
    return jnp.dot(left, right, preferred_element_type=f32)


def dot_nt(left, right):
    return lax.dot_general(left, right, NT, preferred_element_type=f32)


def dot3(left, right):
    left_high, left_low = halves(left)
    right_high, right_low = halves(right)
    return dot(left_high, right_high) + (dot(left_high, right_low) + dot(left_low, right_high))


def turn(cycles):
    part = cycles - jnp.round(cycles)
    square = part * part
    cosine = jnp.full_like(square, COS[-1])
    for factor in COS[-2::-1]:
        cosine = cosine * square + factor
    sine = jnp.full_like(square, SIN[-1])
    for factor in SIN[-2::-1]:
        sine = sine * square + factor
    return cosine, sine * part


def whole(count):
    return [pl.BlockSpec(memory_space=pltpu.VMEM)] * count


def call(kernel, outs, ins, scalars=0, scratch=(), flops=0, name=None):
    specs = [pl.BlockSpec(memory_space=pltpu.SMEM)] * scalars + whole(len(ins) - scalars)
    many = isinstance(outs, (tuple, list))
    size = sum(v.size * v.dtype.itemsize for v in ins)
    return pl.pallas_call(
        kernel,
        out_shape=outs,
        in_specs=specs,
        out_specs=tuple(whole(len(outs))) if many else whole(1)[0],
        scratch_shapes=list(scratch),
        compiler_params=pltpu.CompilerParams(vmem_limit_bytes=56 * 1024 * 1024),
        cost_estimate=pl.CostEstimate(flops=flops, bytes_accessed=size, transcendentals=0),
        name=name,
    )(*ins)


def pack_kernel(where, features, positions, vectors, filters, out):
    place, core = where[0], where[1]
    first = pl.multiple_of(core * 256, 256)
    turned = features[...].T
    chosen = lax.broadcasted_iota(jnp.int32, (32, WIDTH), 1) == (
        lax.broadcasted_iota(jnp.int32, (32, WIDTH), 0) * 16 + place
    )
    picked = lax.dot_general(
        chosen.astype(f32),
        filters[pl.ds(first, 256), :],
        NT,
        precision=lax.Precision.HIGHEST,
        preferred_element_type=f32,
    )
    own = vectors[:, pl.ds(first, 256)].astype(f32)
    coords = positions[...]
    for peer in range(16):
        out[peer, 0:FEATS, :] = turned[peer * FEATS : peer * FEATS + FEATS, :]
        out[peer, AT_POS : AT_POS + 3, :] = coords
        for half in range(2):
            lanes = slice(half * 128, half * 128 + 128)
            out[peer, AT_VEC + 3 * half : AT_VEC + 3 * half + 3, :] = own[:, lanes]
            out[peer, AT_FILTER + 2 * half : AT_FILTER + 2 * half + 2, :] = picked[
                2 * peer : 2 * peer + 2, lanes
            ]
        out[peer, ROWS - 3 : ROWS, :] = jnp.zeros((3, 128), f32)


def gather_filter_kernel(block, out, hot, rows):
    pair = lax.broadcasted_iota(jnp.int32, (128, 128), 0).astype(f32)
    row = lax.broadcasted_iota(jnp.int32, (32, 128), 0)
    third = (row // 2).astype(f32)
    odd = (row % 2) == 1
    for source in range(16):
        for half in range(2):
            at = AT_VEC + 3 * half
            n1 = block[source, at : at + 1, :]
            n2 = block[source, at + 1 : at + 2, :]
            n3 = block[source, at + 2 : at + 3, :]
            negative = (n1 < 0) | ((n1 == 0) & (n2 < 0))
            sign = jnp.where(negative, -1.0, 1.0)
            index = sign * (13.0 * n1 + n2)
            n3 = sign * n3
            index3 = jnp.where(n3 >= 0, n3, 8.0 - n3)
            lanes = slice((2 * source + half) * 128, (2 * source + half) * 128 + 128)
            hot[:, lanes] = (pair == index).astype(f32).astype(bf16)
            at = AT_FILTER + 2 * half
            value = jnp.where(odd, block[source, at + 1 : at + 2, :], block[source, at : at + 1, :])
            match = (third == index3).astype(f32)
            high, low = halves(match * value)
            rows[0:32, lanes] = high
            rows[32:64, lanes] = low
            rows[64:96, lanes] = match.astype(bf16)
    result = dot_nt(rows[...], hot[...])
    out[0:32, :] = result[0:32] + result[32:64]
    out[32:64, :] = result[64:96]


def forward_kernel(block, out, plane_high, plane_low, third_out, left):
    index = lax.broadcasted_iota(jnp.int32, (128, 128), 0).astype(f32)
    n1 = jnp.floor((index + 6.5) * (1.0 / 13.0))
    n2 = index - 13.0 * n1
    n3 = lax.broadcasted_iota(jnp.int32, (8, 128), 0).astype(f32)

    def tile(source, carry):
        lanes = pl.ds(pl.multiple_of(source * 128, 128), 128)
        first = block[source, AT_POS : AT_POS + 1, :]
        second = block[source, AT_POS + 1 : AT_POS + 2, :]
        last = block[source, AT_POS + 2 : AT_POS + 3, :]
        cosine, sine = turn(n1 * first + n2 * second)
        for at, value in ((0, cosine), (128, sine)):
            high, low = halves(value)
            plane_high[at : at + 128, lanes] = high
            plane_low[at : at + 128, lanes] = low
        third = jnp.concatenate(turn(n3 * last), axis=0)
        third_out[:, lanes] = third
        feats = block[source, 0:FEATS, :]
        for at, j in enumerate(USED):
            high, low = halves(third[j : j + 1, :] * feats)
            left[32 * at : 32 * at + 32, lanes] = high
            left[416 + 32 * at : 416 + 32 * at + 32, lanes] = low
        return carry

    lax.fori_loop(0, 16, tile, 0)
    both = dot_nt(left[...], plane_high[...])
    rest = dot_nt(left[0:416, :], plane_low[...])
    result = both[0:416] + (both[416:832] + rest)
    for j in (7, 8, 15):
        out[:, 2 * j : 2 * j + 2, :] = jnp.zeros((16, 2, 256), f32)
    for at, j in enumerate(USED):
        for side in range(2):
            start = 32 * at + 16 * side
            out[:, 2 * j + side, :] = result[start : start + 16, :]


def filter_kernel(parts, weights, out):
    total = parts[0]
    for source in range(1, 16):
        total = total + parts[source]
    cc, sc = total[0:16, 0:128], total[0:16, 128:256]
    cs, ss = total[16:32, 0:128], total[16:32, 128:256]
    plus, minus = weights[0:16, :], weights[16:32, :]
    plus_count, minus_count = weights[32:48, :], weights[48:64, :]
    cos_plus, cos_minus = cc - ss, cc + ss
    sin_plus, sin_minus = sc + cs, sc - cs
    energy = plus_count * (cos_plus * cos_plus + sin_plus * sin_plus)
    energy = energy + minus_count * (cos_minus * cos_minus + sin_minus * sin_minus)
    energy = jnp.sum(energy, axis=1, keepdims=True)
    odd = (lax.broadcasted_iota(jnp.int32, (16, 1), 0) % 2) == 1
    power_odd = jnp.sum(jnp.where(odd, energy, 0.0), axis=0, keepdims=True)
    power_even = jnp.sum(jnp.where(odd, 0.0, energy), axis=0, keepdims=True)
    power = jnp.where(odd, power_odd, power_even)
    scale = lax.rsqrt(power / (2 * KVEC) + epsilon) * (1.0 / 64.0)
    plus, minus = plus * scale, minus * scale
    cos_plus, cos_minus = plus * cos_plus, minus * cos_minus
    sin_plus, sin_minus = plus * sin_plus, minus * sin_minus
    upper = jnp.concatenate([cos_plus + cos_minus, sin_plus + sin_minus], axis=1)
    lower = jnp.concatenate([sin_plus - sin_minus, cos_minus - cos_plus], axis=1)
    both = jnp.concatenate([upper, lower], axis=0)
    for peer in range(16):
        out[peer] = both


def inverse_kernel(block, plane_high, plane_low, third, out, left):
    for at, j in enumerate(USED):
        for side in range(2):
            high, low = halves(block[:, 2 * j + side, :])
            start = 32 * at + 16 * side
            left[start : start + 16, :] = high
            left[416 + start : 416 + start + 16, :] = low

    def tile(step, carry):
        lanes = pl.ds(pl.multiple_of(step * 256, 256), 256)
        high = plane_high[:, lanes]
        both = dot(left[...], high)
        rest = dot(left[0:416, :], plane_low[:, lanes])
        basis = third[:, lanes]
        total = jnp.zeros((FEATS, 256), f32)
        for at, j in enumerate(USED):
            rows = slice(32 * at, 32 * at + 32)
            wide = both[rows] + (both[416 + 32 * at : 448 + 32 * at] + rest[rows])
            total = total + basis[j : j + 1, :] * wide
        out[2 * step] = total[:, 0:128]
        out[2 * step + 1] = total[:, 128:256]
        return carry

    lax.fori_loop(0, 8, tile, 0)


def short_kernel(
    before, own, after, slots, count, distance, w_self, w_neighbour, w_edge, w_message, out,
    left, right, total,
):
    nb_high, nb_low = halves(w_neighbour[...])
    for at, part in enumerate((before, own, after)):
        high, low = halves(part[...])
        projected = dot(high, nb_high) + (dot(high, nb_low) + dot(low, nb_high))
        left[:, at * 128 : at * 128 + 128] = (0.5 * projected).T.astype(bf16)
    edge_high, edge_low = halves(0.5 * w_edge[...])
    blank = jnp.zeros((80, WIDTH), f32)
    edges = jnp.concatenate(
        [edge_high.astype(f32), edge_low.astype(f32), edge_high.astype(f32), blank], axis=0
    )
    left[:, 384:512] = edges.T.astype(bf16)
    mine = (0.5 * dot3(own[...], w_self[...])).T
    right[432:512, :] = jnp.zeros((80, 256), bf16)
    total[...] = jnp.zeros_like(total)
    window = lax.broadcasted_iota(jnp.int32, (384, 128), 0)
    spacing = reach / (RADIAL - 1)
    centers = lax.broadcasted_iota(jnp.int32, (RADIAL, 128), 0).astype(f32) * spacing
    live = count[...]

    def step(pair, carry):
        for side in range(2):
            slot = 2 * pair + side
            lanes = slice(side * 128, side * 128 + 128)
            wanted = slots[pl.ds(slot, 1), :]
            right[0:384, lanes] = (window == wanted).astype(f32).astype(bf16)
            offset = (distance[pl.ds(slot, 1), :] - centers) / spacing
            high, low = halves(jnp.exp(-(offset * offset)))
            right[384:400, lanes] = high
            right[400:416, lanes] = high
            right[416:432, lanes] = low
        wide = dot(left[...], right[...])
        for side in range(2):
            half = wide[:, side * 128 : side * 128 + 128] + mine
            message = half + half * jnp.tanh(half)
            valid = (2 * pair + side < live).astype(f32)
            total[...] += message * valid
        return carry

    lax.fori_loop(0, SLOTS // 2, step, 0)
    summed = total[...].T * (1.0 / SLOTS)
    out[...] = own[...] + dot3(summed, w_message[...])


def update_kernel(block, base, gain, w_up, w_down, out):
    total = base[...] + block[...].reshape(WIDTH, 128).T
    mean = jnp.mean(total * total, axis=1, keepdims=True)
    normed = total * lax.rsqrt(mean + epsilon) * gain[...]
    hidden = dot3(normed, w_up[...])
    hidden = hidden * jax.nn.sigmoid(hidden)
    out[...] = total + dot3(hidden, w_down[...])


def local(
    features, positions, wavevectors, neighbour_slots, neighbour_count, pair_distance,
    w_self, w_neighbour, w_edge, w_message, spec_filter, norm_gain, w_up, w_down,
):
    devices = 1
    for axis in EVERY:
        devices *= lax.axis_size(axis)
    ahead = [(i, i + 1) for i in range(devices - 1)]
    place = lax.axis_index("x") * lax.axis_size("y") + lax.axis_index("y")
    where = jnp.stack([place, lax.axis_index("core")]).astype(jnp.int32)

    packed = call(
        pack_kernel, jax.ShapeDtypeStruct((16, ROWS, 128), f32),
        [where, features, positions, wavevectors, spec_filter], scalars=1, name="pack",
    )
    block = lax.all_to_all(packed, TRADE, 0, 0, tiled=True)
    block, ready = lax.optimization_barrier((block, features))
    before = lax.ppermute(ready, EVERY, ahead)
    after = lax.ppermute(ready, EVERY, [(t, s) for s, t in ahead])
    weights = call(
        gather_filter_kernel, jax.ShapeDtypeStruct((64, 128), f32), [block],
        scratch=[pltpu.VMEM((128, KVEC), bf16), pltpu.VMEM((96, KVEC), bf16)], name="weigh",
    )
    parts, plane_high, plane_low, third = call(
        forward_kernel,
        (
            jax.ShapeDtypeStruct((16, 32, 256), f32),
            jax.ShapeDtypeStruct((256, 2048), bf16),
            jax.ShapeDtypeStruct((256, 2048), bf16),
            jax.ShapeDtypeStruct((16, 2048), f32),
        ),
        [block], scratch=[pltpu.VMEM((832, 2048), bf16)], name="forward",
    )
    parts = lax.all_to_all(parts, TOTAL, 0, 0, tiled=True)
    filtered = call(
        filter_kernel, jax.ShapeDtypeStruct((16, 32, 256), f32), [parts, weights], name="filter",
    )
    filtered, before, after = lax.optimization_barrier((filtered, before, after))
    filtered = lax.all_to_all(filtered, TOTAL, 0, 0, tiled=True)
    beads = call(
        inverse_kernel, jax.ShapeDtypeStruct((16, FEATS, 128), f32),
        [filtered, plane_high, plane_low, third],
        scratch=[pltpu.VMEM((832, 256), bf16)], name="inverse",
    )
    beads = lax.all_to_all(beads, TRADE, 0, 0, tiled=True)
    base = call(
        short_kernel, jax.ShapeDtypeStruct((128, WIDTH), f32),
        [before, features, after, neighbour_slots, neighbour_count.reshape(1, 128), pair_distance,
         w_self, w_neighbour, w_edge, w_message],
        scratch=[
            pltpu.VMEM((WIDTH, 512), bf16),
            pltpu.VMEM((512, 256), bf16),
            pltpu.VMEM((WIDTH, 128), f32),
        ],
        flops=2 * 512 * 512 * 4096, name="short",
    )
    return call(
        update_kernel, jax.ShapeDtypeStruct((128, WIDTH), f32),
        [beads, base, norm_gain.reshape(1, WIDTH), w_up, w_down], name="update",
    )


def solution(mesh):
    fine = Mesh(mesh.devices.reshape(4, 4, 2, 4, 2), EVERY)
    placed = (
        P(EVERY, None),
        P(None, EVERY),
        P(None, ("zh", "zl")),
        P(None, EVERY),
        P(EVERY),
        P(None, EVERY),
        P(),
        P(),
        P(),
        P(),
        P(("zh", "zl"), None),
        P(),
        P(),
        P(),
    )
    return jax.shard_map(
        local, mesh=fine, in_specs=placed, out_specs=P(EVERY, None), check_vma=False
    )
```

```python
import jax
import jax.numpy as jnp
from jax import lax
from jax.experimental import pallas as pl
from jax.experimental.pallas import tpu as pltpu
from jax.sharding import Mesh, PartitionSpec as P


KVEC = 4096
WIDTH = 512
SLOTS = 32
RADIAL = 16
epsilon = 1e-05
reach = 2.5

TRADE = ("core", "zh", "zl")
TOTAL = ("x", "y")
EVERY = ("x", "y", "core", "zh", "zl")
FEATS = 32
AT_POS = 32
AT_VEC = 35
AT_FILTER = 41
ROWS = 48
USED = tuple(range(7)) + tuple(range(9, 15))

SIN = (6.283182792843448, -41.3414193330158, 81.59613740878913, -76.57967400034956,
       41.20368207513971, -12.268761447381701)
COS = (0.9999999890563522, -19.73920449855691, 64.93911741205494, -85.45013861232991,
       60.16762307755092, -25.967568454487537, 6.528613369793176)

bf16 = jnp.bfloat16
f32 = jnp.float32
NT = (((1,), (1,)), ((), ()))


def halves(value):
    high = value.astype(bf16)
    return high, (value - high.astype(f32)).astype(bf16)


def dot(left, right):
    return jnp.dot(left, right, preferred_element_type=f32)


def dot_nt(left, right):
    return lax.dot_general(left, right, NT, preferred_element_type=f32)


def dot3(left, right):
    left_high, left_low = halves(left)
    right_high, right_low = halves(right)
    return dot(left_high, right_high) + (dot(left_high, right_low) + dot(left_low, right_high))


def turn(cycles):
    part = cycles - jnp.round(cycles)
    square = part * part
    cosine = jnp.full_like(square, COS[-1])
    for factor in COS[-2::-1]:
        cosine = cosine * square + factor
    sine = jnp.full_like(square, SIN[-1])
    for factor in SIN[-2::-1]:
        sine = sine * square + factor
    return cosine, sine * part


class Held:
    def __init__(self, source, target, done):
        self.copy = pltpu.make_async_copy(source, target, done)
        self.target = target
        self.waiting = True
        self.copy.start()

    def get(self):
        if self.waiting:
            self.copy.wait()
            self.waiting = False
        return self.target


HBM = pltpu.HBM
VMEM = pltpu.VMEM


def call(kernel, outs, ins, mib, scratch=(), flops=0, copies=0):
    size = sum(v.size * v.dtype.itemsize for v, _ in ins)
    result = pl.pallas_call(
        kernel,
        out_shape=tuple(HBM(v.shape, v.dtype) if space is HBM else v for v, space in outs),
        in_specs=[pl.BlockSpec(memory_space=space) for _, space in ins],
        out_specs=tuple(pl.BlockSpec(memory_space=space) for _, space in outs),
        scratch_shapes=list(scratch) + [pltpu.SemaphoreType.DMA((copies,))] * (copies > 0),
        compiler_params=pltpu.CompilerParams(vmem_limit_bytes=mib * 1024 * 1024),
        cost_estimate=pl.CostEstimate(flops=flops, bytes_accessed=size, transcendentals=0),
    )(*[pltpu.with_memory_space_constraint(v, HBM) if space is HBM else v for v, space in ins])
    return result if len(outs) > 1 else result[0]


def pack_kernel(
    features, positions, vectors, filters, out, features_in, positions_in, vectors_in, filters_in,
    done,
):
    place = lax.axis_index("x") * 4 + lax.axis_index("y")
    first = pl.multiple_of(lax.axis_index("core") * 256, 256)
    filters = Held(filters.at[pl.ds(first, 256)], filters_in, done.at[0])
    features = Held(features, features_in, done.at[1])
    vectors = Held(vectors, vectors_in, done.at[2])
    positions = Held(positions, positions_in, done.at[3])
    chosen = lax.broadcasted_iota(jnp.int32, (32, WIDTH), 1) == (
        lax.broadcasted_iota(jnp.int32, (32, WIDTH), 0) * 16 + place
    )
    chosen = chosen.astype(f32).astype(bf16)
    high, low = halves(filters.get()[...])
    picked = dot_nt(chosen, high) + dot_nt(chosen, low)
    turned = features.get()[...].T
    own = vectors.get()[:, pl.ds(first, 256)].astype(f32)
    positions = positions.get()
    coords = positions[...]
    for peer in range(16):
        out[peer, 0:FEATS, :] = turned[peer * FEATS : peer * FEATS + FEATS, :]
        out[peer, AT_POS : AT_POS + 3, :] = coords
        for half in range(2):
            lanes = slice(half * 128, half * 128 + 128)
            out[peer, AT_VEC + 3 * half : AT_VEC + 3 * half + 3, :] = own[:, lanes]
            out[peer, AT_FILTER + 2 * half : AT_FILTER + 2 * half + 2, :] = picked[
                2 * peer : 2 * peer + 2, lanes
            ]
        out[peer, ROWS - 3 : ROWS, :] = jnp.zeros((3, 128), f32)


def weigh_kernel(block, out_far, third_far, hot, rows, out, third_out, done):
    number = lax.broadcasted_iota(jnp.int32, (8, 128), 0).astype(f32)
    for source in range(16):
        lanes = slice(source * 128, source * 128 + 128)
        cosine, sine = turn(number * block[source, AT_POS + 2 : AT_POS + 3, :])
        third_out[0:8, lanes] = cosine
        third_out[8:16, lanes] = sine
    third_copy = pltpu.make_async_copy(third_out, third_far, done.at[0])
    third_copy.start()
    pair = lax.broadcasted_iota(jnp.int32, (128, 128), 0).astype(f32)
    row = lax.broadcasted_iota(jnp.int32, (32, 128), 0)
    third = (row // 2).astype(f32)
    odd = (row % 2) == 1
    for source in range(16):
        for half in range(2):
            at = AT_VEC + 3 * half
            n1 = block[source, at : at + 1, :]
            n2 = block[source, at + 1 : at + 2, :]
            n3 = block[source, at + 2 : at + 3, :]
            negative = (n1 < 0) | ((n1 == 0) & (n2 < 0))
            sign = jnp.where(negative, -1.0, 1.0)
            n2 = sign * n2
            n3 = sign * n3
            index = 16.0 * (sign * n1) + jnp.where(n2 >= 0, n2, 8.0 - n2)
            index3 = jnp.where(n3 >= 0, n3, 8.0 - n3)
            lanes = slice((2 * source + half) * 128, (2 * source + half) * 128 + 128)
            hot[:, lanes] = (pair == index).astype(f32).astype(bf16)
            at = AT_FILTER + 2 * half
            value = jnp.where(odd, block[source, at + 1 : at + 2, :], block[source, at : at + 1, :])
            match = (third == index3).astype(f32)
            high, low = halves(match * value)
            rows[0:32, lanes] = high
            rows[32:64, lanes] = low
            rows[64:96, lanes] = match.astype(bf16)
    result = dot_nt(rows[...], hot[...])
    out[0:32, :] = result[0:32] + result[32:64]
    out[32:64, :] = result[64:96]
    copy = pltpu.make_async_copy(out, out_far, done.at[1])
    copy.start()
    third_copy.wait()
    copy.wait()


def forward_kernel(block, out_far, plane, left, out, done):
    number = lax.broadcasted_iota(jnp.int32, (8, 128), 0).astype(f32)
    blank = jnp.zeros((16, 2048), bf16)
    for at in range(112, 768, 128):
        plane[at : at + 16, :] = blank

    def tile(source, carry):
        lanes = pl.ds(pl.multiple_of(source * 128, 128), 128)
        cos1, sin1 = turn(number * block[source, AT_POS : AT_POS + 1, :])
        cos2, sin2 = turn(number * block[source, AT_POS + 1 : AT_POS + 2, :])
        cos3, sin3 = turn(number * block[source, AT_POS + 2 : AT_POS + 3, :])
        for n1 in range(7):
            cosine, sine = cos1[n1 : n1 + 1, :], sin1[n1 : n1 + 1, :]
            cc, ss = cosine * cos2, sine * sin2
            sc, cs = sine * cos2, cosine * sin2
            wave = jnp.concatenate([cc - ss, cc + ss], axis=0)
            high, low = halves(wave)
            at = 16 * n1
            plane[at : at + 16, lanes] = high
            plane[256 + at : 272 + at, lanes] = low
            plane[512 + at : 528 + at, lanes] = high
            wave = jnp.concatenate([sc + cs, sc - cs], axis=0)
            high, low = halves(wave)
            at = 128 + 16 * n1
            plane[at : at + 16, lanes] = high
            plane[256 + at : 272 + at, lanes] = low
            plane[512 + at : 528 + at, lanes] = high
        feats = block[source, 0:FEATS, :]
        for at, j in enumerate(USED):
            basis = cos3[j : j + 1, :] if j < 8 else sin3[j - 8 : j - 7, :]
            high, low = halves(basis * feats)
            left[32 * at : 32 * at + 32, lanes] = high
            left[416 + 32 * at : 416 + 32 * at + 32, lanes] = low
        return carry

    lax.fori_loop(0, 16, tile, 0, unroll=2)
    both = dot_nt(left[...], plane[0:256, :])
    rest = dot_nt(left[0:416, :], plane[256:512, :])
    result = both[0:416] + (both[416:832] + rest)
    for half in range(2):
        lanes = slice(128 * half, 128 * half + 128)
        for row in (14, 15, 16, 17, 30, 31):
            out[pl.ds(32 * half + row, 16, stride=64), :] = jnp.zeros((16, 128), f32)
        for at, j in enumerate(USED):
            for side in range(2):
                start = 32 * at + 16 * side
                rows = pl.ds(32 * half + 2 * j + side, 16, stride=64)
                out[rows, :] = result[start : start + 16, lanes]
    copy = pltpu.make_async_copy(out, out_far, done.at[0])
    copy.start()
    copy.wait()


def filter_kernel(parts_far, weights_far, out_far, parts, weights_in, out, done):
    fetches = [
        Held(parts_far.at[pl.ds(4 * i, 4)], parts.at[pl.ds(4 * i, 4)], done.at[i])
        for i in range(4)
    ]
    weights = Held(weights_far, weights_in, done.at[4])
    total = jnp.zeros((64, 128), f32)
    for i in range(4):
        fetches[i].get()
        for source in range(4 * i, 4 * i + 4):
            total = total + parts[source]
    weights = weights.get()
    cc, cs, sc, ss = total[0:16], total[16:32], total[32:48], total[48:64]
    plus, minus = weights[0:16, :], weights[16:32, :]
    plus_count, minus_count = weights[32:48, :], weights[48:64, :]
    cos_plus, cos_minus = cc - ss, cc + ss
    sin_plus, sin_minus = sc + cs, sc - cs
    energy = plus_count * (cos_plus * cos_plus + sin_plus * sin_plus)
    energy = energy + minus_count * (cos_minus * cos_minus + sin_minus * sin_minus)
    energy = jnp.sum(energy, axis=1, keepdims=True)
    odd = (lax.broadcasted_iota(jnp.int32, (16, 1), 0) % 2) == 1
    power_odd = jnp.sum(jnp.where(odd, energy, 0.0), axis=0, keepdims=True)
    power_even = jnp.sum(jnp.where(odd, 0.0, energy), axis=0, keepdims=True)
    power = jnp.where(odd, power_odd, power_even)
    scale = lax.rsqrt(power / (2 * KVEC) + epsilon) * (1.0 / 64.0)
    plus, minus = plus * scale, minus * scale
    cos_plus, cos_minus = plus * cos_plus, minus * cos_minus
    sin_plus, sin_minus = plus * sin_plus, minus * sin_minus
    out[0:16, :] = cos_plus + cos_minus
    out[16:32, :] = sin_plus - sin_minus
    out[32:48, :] = sin_plus + sin_minus
    out[48:64, :] = cos_minus - cos_plus
    copies = [
        pltpu.make_async_copy(out, out_far.at[peer], done.at[5 + peer]) for peer in range(16)
    ]
    for copy in copies:
        copy.start()
    for copy in copies:
        copy.wait()


def inverse_kernel(block_far, third_far, plane, out_far, left, block_in, third_in, out, done):
    block = Held(block_far, block_in, done.at[8])
    third = Held(third_far, third_in, done.at[9]).get()
    block = block.get()
    for at, j in enumerate(USED):
        for side in range(2):
            start = 32 * at + 16 * side
            for half in range(2):
                rows = pl.ds(32 * half + 2 * j + side, 16, stride=64)
                high, low = halves(block[rows, :])
                lane = 128 * half
                left[start : start + 16, lane : lane + 128] = high
                left[start : start + 16, 256 + lane : 384 + lane] = high
                left[start : start + 16, 512 + lane : 640 + lane] = low

    def send(step):
        rows = pl.ds(2 * step, 2)
        return pltpu.make_async_copy(out.at[rows], out_far.at[rows], done.at[step])

    def tile(step, carry):
        lanes = pl.ds(pl.multiple_of(step * 256, 256), 256)
        wide = dot(left[...], plane[:, lanes])
        basis = third[:, lanes]
        total = jnp.zeros((FEATS, 256), f32)
        for at, j in enumerate(USED):
            total = total + basis[j : j + 1, :] * wide[32 * at : 32 * at + 32]
        out[2 * step] = total[:, 0:128]
        out[2 * step + 1] = total[:, 128:256]
        send(step).start()
        return carry

    lax.fori_loop(0, 8, tile, 0, unroll=2)
    for step in range(8):
        send(step).wait()


def run_slots(low, high, slots, count, distance, left, mine, right, total):
    right[432:512, :] = jnp.zeros((80, 512), bf16)
    window = lax.broadcasted_iota(jnp.int32, (384, 128), 0)
    spacing = reach / (RADIAL - 1)
    centers = lax.broadcasted_iota(jnp.int32, (RADIAL, 128), 0).astype(f32) * spacing
    live = count[...]

    def step(quad, carry):
        for pair in range(2):
            for side in range(2):
                slot = 4 * quad + 2 * pair + side
                lanes = slice(256 * pair + side * 128, 256 * pair + side * 128 + 128)
                wanted = slots[pl.ds(slot, 1), :]
                hot = (window == wanted).astype(f32).astype(bf16)
                right[0:384, lanes] = hot
                right[512:896, lanes] = hot
                offset = (distance[pl.ds(slot, 1), :] - centers) / spacing
                upper, lower = halves(jnp.exp(-(offset * offset)))
                right[384:400, lanes] = upper
                right[400:416, lanes] = upper
                right[416:432, lanes] = lower
            wide = dot(left[...], right[:, 256 * pair : 256 * pair + 256])
            added = total[...]
            for side in range(2):
                half = wide[:, side * 128 : side * 128 + 128] + mine[...]
                message = half + half * jnp.tanh(half)
                valid = (4 * quad + 2 * pair + side < live).astype(f32)
                added = added + message * valid
            total[...] = added
        return carry

    lax.fori_loop(low, high, step, 0)


FIRST_QUADS = 2


def ready_kernel(
    before, own, after, w_self, w_neighbour, w_edge, slots, count, distance,
    left_far, mine_far, total_far,
    before_in, own_in, after_in, w_self_in, w_neighbour_in, w_edge_in, slots_in, count_in,
    distance_in, left, mine, total, right, done,
):
    w_neighbour = Held(w_neighbour, w_neighbour_in, done.at[0])
    parts = [
        Held(own, own_in, done.at[1]),
        Held(before, before_in, done.at[2]),
        Held(after, after_in, done.at[3]),
    ]
    w_self = Held(w_self, w_self_in, done.at[4])
    w_edge = Held(w_edge, w_edge_in, done.at[5])
    slots = Held(slots, slots_in, done.at[6])
    count = Held(count, count_in, done.at[7])
    distance = Held(distance, distance_in, done.at[8])
    nb_high, nb_low = halves(0.5 * w_neighbour.get()[...])
    for at, part in zip((128, 0, 256), parts):
        high, low = halves(part.get()[...])
        projected = dot(high, nb_high) + (dot(high, nb_low) + dot(low, nb_high))
        high, low = halves(projected.T)
        left[:, at : at + 128] = high
        left[:, 512 + at : 640 + at] = low
    edge_high, edge_low = halves(0.5 * w_edge.get()[...])
    edge_high, edge_low = edge_high.astype(f32), edge_low.astype(f32)
    blank = jnp.zeros((80, WIDTH), f32)
    edges = jnp.concatenate([edge_high, edge_low, edge_high, blank], axis=0)
    left[:, 384:512] = edges.T.astype(bf16)
    left_copy = pltpu.make_async_copy(left, left_far, done.at[9])
    left_copy.start()
    mine[...] = (0.5 * dot3(own_in[...], w_self.get()[...])).T
    mine_copy = pltpu.make_async_copy(mine, mine_far, done.at[10])
    mine_copy.start()
    total[...] = jnp.zeros_like(total)
    run_slots(
        0, FIRST_QUADS, slots.get(), count.get(), distance.get(), left, mine, right, total
    )
    total_copy = pltpu.make_async_copy(total, total_far, done.at[11])
    total_copy.start()
    left_copy.wait()
    mine_copy.wait()
    total_copy.wait()


def short_kernel(
    own, slots, count, distance, left, mine, total, w_message, out,
    own_in, slots_in, count_in, distance_in, left_in, mine_in, total_in, w_message_in, right, done,
):
    left = Held(left, left_in, done.at[0])
    slots = Held(slots, slots_in, done.at[1])
    count = Held(count, count_in, done.at[2])
    distance = Held(distance, distance_in, done.at[3])
    mine = Held(mine, mine_in, done.at[4])
    total = Held(total, total_in, done.at[5])
    w_message = Held(w_message, w_message_in, done.at[6])
    own = Held(own, own_in, done.at[7])
    run_slots(
        FIRST_QUADS, SLOTS // 4, slots.get(), count.get(), distance.get(), left.get(),
        mine.get(), right, total.get(),
    )
    summed = total_in[...].T * (1.0 / SLOTS)
    out[...] = own.get()[...] + dot3(summed, w_message.get()[...])


def update_kernel(block, base, gain, w_up, w_down, out):
    total = base[...] + block[...].reshape(WIDTH, 128).T
    mean = jnp.mean(total * total, axis=1, keepdims=True)
    normed = total * lax.rsqrt(mean + epsilon) * gain[...]
    hidden = dot3(normed, w_up[...])
    hidden = hidden * jax.nn.sigmoid(hidden)
    out[...] = total + dot3(hidden, w_down[...])


def swap(value, axes):
    return lax.all_to_all(value, axes, 0, 0, tiled=True)


def shape(*dims, dtype=f32):
    return jax.ShapeDtypeStruct(dims, dtype)


def local(
    features, positions, wavevectors, neighbour_slots, neighbour_count, pair_distance,
    w_self, w_neighbour, w_edge, w_message, spec_filter, norm_gain, w_up, w_down,
):
    devices = 1
    for axis in EVERY:
        devices *= lax.axis_size(axis)
    ahead = [(i, i + 1) for i in range(devices - 1)]

    packed = call(
        pack_kernel, [(shape(16, ROWS, 128), VMEM)],
        [(features, HBM), (positions, HBM), (wavevectors, HBM), (spec_filter, HBM)], 8,
        scratch=[
            VMEM((128, WIDTH), f32), VMEM((3, 128), f32), VMEM((3, 512), jnp.int32),
            VMEM((256, WIDTH), f32),
        ],
        copies=4,
    )
    block = swap(packed, TRADE)
    block, ready = lax.optimization_barrier((block, features))
    before = lax.ppermute(ready, EVERY, ahead)
    after = lax.ppermute(ready, EVERY, [(t, s) for s, t in ahead])
    parts, plane = call(
        forward_kernel,
        [(shape(1024, 128), HBM), (shape(768, 2048, dtype=bf16), VMEM)],
        [(block, VMEM)], 16,
        scratch=[VMEM((832, 2048), bf16), VMEM((1024, 128), f32)],
        flops=10**9, copies=1,
    )
    parts = swap(parts.reshape(16, 64, 128), TOTAL)
    weights, third = call(
        weigh_kernel, [(shape(64, 128), HBM), (shape(16, 2048), HBM)], [(block, VMEM)], 8,
        scratch=[
            VMEM((128, KVEC), bf16), VMEM((96, KVEC), bf16), VMEM((64, 128), f32),
            VMEM((16, 2048), f32),
        ],
        flops=10**9, copies=2,
    )
    filtered = call(
        filter_kernel, [(shape(16, 64, 128), HBM)], [(parts, HBM), (weights, HBM)], 4,
        scratch=[VMEM((16, 64, 128), f32), VMEM((64, 128), f32), VMEM((64, 128), f32)],
        copies=21,
    )
    filtered = swap(filtered, TOTAL)
    lists = [
        (neighbour_slots, HBM), (neighbour_count.reshape(1, 128), HBM), (pair_distance, HBM),
    ]
    lists_in = [VMEM((32, 128), jnp.int32), VMEM((1, 128), jnp.int32), VMEM((32, 128), f32)]
    left, mine, total = call(
        ready_kernel,
        [(shape(WIDTH, 896, dtype=bf16), HBM), (shape(WIDTH, 128), HBM),
         (shape(WIDTH, 128), HBM)],
        [(before, HBM), (features, HBM), (after, HBM), (w_self, HBM), (w_neighbour, HBM),
         (w_edge, HBM)] + lists, 16,
        scratch=[
            VMEM((128, WIDTH), f32), VMEM((128, WIDTH), f32), VMEM((128, WIDTH), f32),
            VMEM((WIDTH, WIDTH), f32), VMEM((WIDTH, WIDTH), f32), VMEM((RADIAL, WIDTH), f32),
        ] + lists_in + [
            VMEM((WIDTH, 896), bf16), VMEM((WIDTH, 128), f32), VMEM((WIDTH, 128), f32),
            VMEM((896, 512), bf16),
        ],
        flops=2 * 10**9, copies=12,
    )
    beads = call(
        inverse_kernel, [(shape(16, FEATS, 128), HBM)],
        [(filtered.reshape(1024, 128), HBM), (third, HBM), (plane, VMEM)], 8,
        scratch=[
            VMEM((416, 768), bf16), VMEM((1024, 128), f32), VMEM((16, 2048), f32),
            VMEM((16, FEATS, 128), f32),
        ],
        flops=10**9, copies=10,
    )
    beads = swap(beads, TRADE)
    base = call(
        short_kernel, [(shape(128, WIDTH), VMEM)],
        [(features, HBM)] + lists + [(left, HBM), (mine, HBM), (total, HBM), (w_message, HBM)],
        12,
        scratch=[VMEM((128, WIDTH), f32)] + lists_in + [
            VMEM((WIDTH, 896), bf16), VMEM((WIDTH, 128), f32), VMEM((WIDTH, 128), f32),
            VMEM((WIDTH, WIDTH), f32), VMEM((896, 512), bf16),
        ],
        flops=2 * 896 * 512 * 4096, copies=8,
    )
    return call(
        update_kernel, [(shape(128, WIDTH), VMEM)],
        [(beads, VMEM), (base, VMEM), (norm_gain.reshape(1, WIDTH), VMEM), (w_up, VMEM),
         (w_down, VMEM)], 12,
    )


def solution(mesh):
    fine = Mesh(mesh.devices.reshape(4, 4, 2, 4, 2), EVERY)
    placed = (
        P(EVERY, None),
        P(None, EVERY),
        P(None, ("zh", "zl")),
        P(None, EVERY),
        P(EVERY),
        P(None, EVERY),
        P(),
        P(),
        P(),
        P(),
        P(("zh", "zl"), None),
        P(),
        P(),
        P(),
    )

    return jax.shard_map(
        local, mesh=fine, in_specs=placed, out_specs=P(EVERY, None), check_vma=False
    )
```

```python
import jax
import jax.numpy as jnp
from jax import lax
from jax.experimental import pallas as pl
from jax.experimental.pallas import tpu as pltpu
from jax.sharding import Mesh, PartitionSpec as P


KVEC = 4096
WIDTH = 512
SLOTS = 32
RADIAL = 16
epsilon = 1e-05
reach = 2.5

TRADE = ("core", "zh", "zl")
TOTAL = ("x", "y")
EVERY = ("x", "y", "core", "zh", "zl")
FEATS = 32
AT_POS = 32
AT_VEC = 35
AT_FILTER = 41
ROWS = 48
PART = 56
USED = tuple(range(7)) + tuple(range(9, 15))

SIN = (6.283182792843448, -41.3414193330158, 81.59613740878913, -76.57967400034956,
       41.20368207513971, -12.268761447381701)
COS = (0.9999999890563522, -19.73920449855691, 64.93911741205494, -85.45013861232991,
       60.16762307755092, -25.967568454487537, 6.528613369793176)

bf16 = jnp.bfloat16
f32 = jnp.float32
NT = (((1,), (1,)), ((), ()))


def halves(value):
    high = value.astype(bf16)
    return high, (value - high.astype(f32)).astype(bf16)


def dot(left, right):
    return jnp.dot(left, right, preferred_element_type=f32)


def dot_nt(left, right):
    return lax.dot_general(left, right, NT, preferred_element_type=f32)


def dot3(left, right):
    left_high, left_low = halves(left)
    right_high, right_low = halves(right)
    return dot(left_high, right_high) + (dot(left_high, right_low) + dot(left_low, right_high))


def turn(cycles):
    part = cycles - jnp.round(cycles)
    square = part * part
    cosine = jnp.full_like(square, COS[-1])
    for factor in COS[-2::-1]:
        cosine = cosine * square + factor
    sine = jnp.full_like(square, SIN[-1])
    for factor in SIN[-2::-1]:
        sine = sine * square + factor
    return cosine, sine * part


class Held:
    def __init__(self, source, target, done):
        self.copy = pltpu.make_async_copy(source, target, done)
        self.target = target
        self.waiting = True
        self.copy.start()

    def get(self):
        if self.waiting:
            self.copy.wait()
            self.waiting = False
        return self.target


HBM = pltpu.HBM
VMEM = pltpu.VMEM


def call(kernel, outs, ins, mib, scratch=(), flops=0, copies=0):
    size = sum(v.size * v.dtype.itemsize for v, _ in ins)
    result = pl.pallas_call(
        kernel,
        out_shape=tuple(HBM(v.shape, v.dtype) if space is HBM else v for v, space in outs),
        in_specs=[pl.BlockSpec(memory_space=space) for _, space in ins],
        out_specs=tuple(pl.BlockSpec(memory_space=space) for _, space in outs),
        scratch_shapes=list(scratch) + [pltpu.SemaphoreType.DMA((copies,))] * (copies > 0),
        compiler_params=pltpu.CompilerParams(vmem_limit_bytes=mib * 1024 * 1024),
        cost_estimate=pl.CostEstimate(flops=flops, bytes_accessed=size, transcendentals=0),
    )(*[pltpu.with_memory_space_constraint(v, HBM) if space is HBM else v for v, space in ins])
    return result if len(outs) > 1 else result[0]


def pack_kernel(
    features, positions, vectors, filters, out, features_in, positions_in, vectors_in, filters_in,
    done,
):
    place = lax.axis_index("x") * 4 + lax.axis_index("y")
    first = pl.multiple_of(lax.axis_index("core") * 256, 256)
    filters = Held(filters.at[pl.ds(first, 256)], filters_in, done.at[0])
    features = Held(features, features_in, done.at[1])
    vectors = Held(vectors, vectors_in, done.at[2])
    positions = Held(positions, positions_in, done.at[3])
    chosen = lax.broadcasted_iota(jnp.int32, (32, WIDTH), 1) == (
        lax.broadcasted_iota(jnp.int32, (32, WIDTH), 0) * 16 + place
    )
    chosen = chosen.astype(f32).astype(bf16)
    high, low = halves(filters.get()[...])
    picked = dot_nt(chosen, high) + dot_nt(chosen, low)
    turned = features.get()[...].T
    own = vectors.get()[:, pl.ds(first, 256)].astype(f32)
    positions = positions.get()
    coords = positions[...]
    for peer in range(16):
        out[peer, 0:FEATS, :] = turned[peer * FEATS : peer * FEATS + FEATS, :]
        out[peer, AT_POS : AT_POS + 3, :] = coords
        for half in range(2):
            lanes = slice(half * 128, half * 128 + 128)
            out[peer, AT_VEC + 3 * half : AT_VEC + 3 * half + 3, :] = own[:, lanes]
            out[peer, AT_FILTER + 2 * half : AT_FILTER + 2 * half + 2, :] = picked[
                2 * peer : 2 * peer + 2, lanes
            ]
        out[peer, ROWS - 3 : ROWS, :] = jnp.zeros((3, 128), f32)


def weigh_kernel(block, out_far, third_far, hot, rows, out, third_out, done):
    number = lax.broadcasted_iota(jnp.int32, (8, 128), 0).astype(f32)
    for source in range(16):
        lanes = slice(source * 128, source * 128 + 128)
        cosine, sine = turn(number * block[source, AT_POS + 2 : AT_POS + 3, :])
        third_out[0:8, lanes] = cosine
        third_out[8:16, lanes] = sine
    third_copy = pltpu.make_async_copy(third_out, third_far, done.at[0])
    third_copy.start()
    pair = lax.broadcasted_iota(jnp.int32, (128, 128), 0).astype(f32)
    row = lax.broadcasted_iota(jnp.int32, (32, 128), 0)
    third = (row // 2).astype(f32)
    odd = (row % 2) == 1
    for source in range(16):
        for half in range(2):
            at = AT_VEC + 3 * half
            n1 = block[source, at : at + 1, :]
            n2 = block[source, at + 1 : at + 2, :]
            n3 = block[source, at + 2 : at + 3, :]
            negative = (n1 < 0) | ((n1 == 0) & (n2 < 0))
            sign = jnp.where(negative, -1.0, 1.0)
            n2 = sign * n2
            n3 = sign * n3
            index = 16.0 * (sign * n1) + jnp.where(n2 >= 0, n2, 8.0 - n2)
            index3 = jnp.where(n3 >= 0, n3, 8.0 - n3)
            lanes = slice((2 * source + half) * 128, (2 * source + half) * 128 + 128)
            hot[:, lanes] = (pair == index).astype(f32).astype(bf16)
            at = AT_FILTER + 2 * half
            value = jnp.where(odd, block[source, at + 1 : at + 2, :], block[source, at : at + 1, :])
            match = (third == index3).astype(f32)
            high, low = halves(match * value)
            rows[0:32, lanes] = high
            rows[32:64, lanes] = low
            rows[64:96, lanes] = match.astype(bf16)
    result = dot_nt(rows[...], hot[...])
    out[0:32, :] = result[0:32] + result[32:64]
    out[32:64, :] = result[64:96]
    copy = pltpu.make_async_copy(out, out_far, done.at[1])
    copy.start()
    third_copy.wait()
    copy.wait()


def forward_kernel(block, out_far, plane, left, out, done):
    number = lax.broadcasted_iota(jnp.int32, (8, 128), 0).astype(f32)
    blank = jnp.zeros((16, 2048), bf16)
    for at in range(112, 512, 128):
        plane[at : at + 16, :] = blank

    for source in range(16):
        lanes = slice(source * 128, source * 128 + 128)
        cos1, sin1 = turn(number * block[source, AT_POS : AT_POS + 1, :])
        cos2, sin2 = turn(number * block[source, AT_POS + 1 : AT_POS + 2, :])
        cos3, sin3 = turn(number * block[source, AT_POS + 2 : AT_POS + 3, :])
        for n1 in range(7):
            cosine, sine = cos1[n1 : n1 + 1, :], sin1[n1 : n1 + 1, :]
            cc, ss = cosine * cos2, sine * sin2
            sc, cs = sine * cos2, cosine * sin2
            wave = jnp.concatenate([cc - ss, cc + ss], axis=0)
            high, low = halves(wave)
            at = 16 * n1
            plane[at : at + 16, lanes] = high
            plane[256 + at : 272 + at, lanes] = low
            wave = jnp.concatenate([sc + cs, sc - cs], axis=0)
            high, low = halves(wave)
            at = 128 + 16 * n1
            plane[at : at + 16, lanes] = high
            plane[256 + at : 272 + at, lanes] = low
        feats = block[source, 0:FEATS, :]
        for at, j in enumerate(USED):
            basis = cos3[j : j + 1, :] if j < 8 else sin3[j - 8 : j - 7, :]
            high, low = halves(basis * feats)
            left[32 * at : 32 * at + 32, lanes] = high
            left[416 + 32 * at : 416 + 32 * at + 32, lanes] = low

    wide, tall = [], []
    for chunk in range(8):
        lanes = slice(chunk * 256, chunk * 256 + 256)
        wide += [left[0:416, lanes], left[0:416, lanes], left[416:832, lanes]]
        tall += [plane[0:256, lanes], plane[256:512, lanes], plane[0:256, lanes]]
    result = dot_nt(jnp.concatenate(wide, axis=1), jnp.concatenate(tall, axis=1))
    for half in range(2):
        lanes = slice(128 * half, 128 * half + 128)
        for row in (52, 53):
            out[pl.ds(2 * half + row, 16, stride=PART), :] = jnp.zeros((16, 128), f32)
        for at, j in enumerate(USED):
            for side in range(2):
                start = 32 * at + 16 * side
                rows = pl.ds(26 * half + 2 * at + side, 16, stride=PART)
                out[rows, :] = result[start : start + 16, lanes]
    copy = pltpu.make_async_copy(out, out_far, done.at[0])
    copy.start()
    copy.wait()


def filter_kernel(parts, weights_far, out_far, weights_in, out, done):
    weights = Held(weights_far, weights_in, done.at[16])
    total = parts[0]
    for source in range(1, 16):
        total = total + parts[source]
    weights = weights.get()
    row = lax.broadcasted_iota(jnp.int32, (16, 128), 0)
    cc, sc = total[0:16], total[26:42]
    cs = jnp.where(row < 2, 0.0, total[12:28])
    ss = jnp.where(row < 2, 0.0, total[38:54])
    plus, minus = weights[0:16, :], weights[16:32, :]
    plus_count, minus_count = weights[32:48, :], weights[48:64, :]
    cos_plus, cos_minus = cc - ss, cc + ss
    sin_plus, sin_minus = sc + cs, sc - cs
    energy = plus_count * (cos_plus * cos_plus + sin_plus * sin_plus)
    energy = energy + minus_count * (cos_minus * cos_minus + sin_minus * sin_minus)
    energy = jnp.sum(energy, axis=1, keepdims=True)
    odd = (lax.broadcasted_iota(jnp.int32, (16, 1), 0) % 2) == 1
    power_odd = jnp.sum(jnp.where(odd, energy, 0.0), axis=0, keepdims=True)
    power_even = jnp.sum(jnp.where(odd, 0.0, energy), axis=0, keepdims=True)
    power = jnp.where(odd, power_odd, power_even)
    scale = lax.rsqrt(power / (2 * KVEC) + epsilon) * (1.0 / 64.0)
    plus, minus = plus * scale, minus * scale
    cos_plus, cos_minus = plus * cos_plus, minus * cos_minus
    sin_plus, sin_minus = plus * sin_plus, minus * sin_minus
    out[0:14, :] = (cos_plus + cos_minus)[0:14]
    out[14:26, :] = (sin_plus - sin_minus)[2:14]
    out[26:40, :] = (sin_plus + sin_minus)[0:14]
    out[40:52, :] = (cos_minus - cos_plus)[2:14]
    out[52:56, :] = jnp.zeros((4, 128), f32)
    copies = [
        pltpu.make_async_copy(out, out_far.at[peer], done.at[peer]) for peer in range(16)
    ]
    for copy in copies:
        copy.start()
    for copy in copies:
        copy.wait()


def inverse_kernel(block, third_far, plane, out_far, left, third_in, out, done):
    third = Held(third_far, third_in, done.at[8])
    for at, j in enumerate(USED):
        for side in range(2):
            start = 32 * at + 16 * side
            for half in range(2):
                rows = pl.ds(26 * half + 2 * at + side, 16, stride=PART)
                high, low = halves(block[rows, :])
                lane = 128 * half
                left[start : start + 16, lane : lane + 128] = high
                left[start : start + 16, 256 + lane : 384 + lane] = low

    third = third.get()

    def send(step):
        rows = pl.ds(2 * step, 2)
        return pltpu.make_async_copy(out.at[rows], out_far.at[rows], done.at[step])

    def tile(step, carry):
        lanes = pl.ds(pl.multiple_of(step * 256, 256), 256)
        upper, lower = plane[0:256, lanes], plane[256:512, lanes]
        wide = dot(
            jnp.concatenate([left[:, 0:256], left[:, 0:256], left[:, 256:512]], axis=1),
            jnp.concatenate([upper, lower, upper], axis=0),
        )
        basis = third[:, lanes]
        total = jnp.zeros((FEATS, 256), f32)
        for at, j in enumerate(USED):
            total = total + basis[j : j + 1, :] * wide[32 * at : 32 * at + 32]
        out[2 * step] = total[:, 0:128]
        out[2 * step + 1] = total[:, 128:256]
        send(step).start()
        return carry

    lax.fori_loop(0, 8, tile, 0, unroll=8)
    for step in range(8):
        send(step).wait()


def run_slots(low, high, slots, count, distance, left, mine, right, total):
    right[432:512, :] = jnp.zeros((80, 512), bf16)
    window = lax.broadcasted_iota(jnp.int32, (384, 128), 0)
    spacing = reach / (RADIAL - 1)
    centers = lax.broadcasted_iota(jnp.int32, (RADIAL, 128), 0).astype(f32) * spacing
    live = count[...]

    def step(quad, carry):
        for pair in range(2):
            for side in range(2):
                slot = 4 * quad + 2 * pair + side
                lanes = slice(256 * pair + side * 128, 256 * pair + side * 128 + 128)
                wanted = slots[pl.ds(slot, 1), :]
                hot = (window == wanted).astype(f32).astype(bf16)
                right[0:384, lanes] = hot
                right[512:896, lanes] = hot
                offset = (distance[pl.ds(slot, 1), :] - centers) / spacing
                upper, lower = halves(jnp.exp(-(offset * offset)))
                right[384:400, lanes] = upper
                right[400:416, lanes] = upper
                right[416:432, lanes] = lower
            wide = dot(left[...], right[:, 256 * pair : 256 * pair + 256])
            added = total[...]
            for side in range(2):
                half = wide[:, side * 128 : side * 128 + 128] + mine[...]
                message = half + half * jnp.tanh(half)
                valid = (4 * quad + 2 * pair + side < live).astype(f32)
                added = added + message * valid
            total[...] = added
        return carry

    lax.fori_loop(low, high, step, 0)


FIRST_QUADS = 2


def ready_kernel(
    before, own, after, w_self, w_neighbour, w_edge, slots, count, distance,
    left_far, mine_far, total_far,
    own_in, w_self_in, w_neighbour_in, w_edge_in, slots_in, count_in,
    distance_in, left, mine, total, right, done,
):
    w_neighbour = Held(w_neighbour, w_neighbour_in, done.at[0])
    own = Held(own, own_in, done.at[1])
    w_self = Held(w_self, w_self_in, done.at[4])
    w_edge = Held(w_edge, w_edge_in, done.at[5])
    slots = Held(slots, slots_in, done.at[6])
    count = Held(count, count_in, done.at[7])
    distance = Held(distance, distance_in, done.at[8])
    nb_high, nb_low = halves(0.5 * w_neighbour.get()[...])
    for at, part in ((0, before), (256, after), (128, own.get())):
        high, low = halves(part[...])
        projected = dot(high, nb_high) + (dot(high, nb_low) + dot(low, nb_high))
        high, low = halves(projected.T)
        left[:, at : at + 128] = high
        left[:, 512 + at : 640 + at] = low
    edge_high, edge_low = halves(0.5 * w_edge.get()[...])
    edge_high, edge_low = edge_high.astype(f32), edge_low.astype(f32)
    blank = jnp.zeros((80, WIDTH), f32)
    edges = jnp.concatenate([edge_high, edge_low, edge_high, blank], axis=0)
    left[:, 384:512] = edges.T.astype(bf16)
    left_copy = pltpu.make_async_copy(left, left_far, done.at[9])
    left_copy.start()
    mine[...] = (0.5 * dot3(own_in[...], w_self.get()[...])).T
    mine_copy = pltpu.make_async_copy(mine, mine_far, done.at[10])
    mine_copy.start()
    total[...] = jnp.zeros_like(total)
    run_slots(
        0, FIRST_QUADS, slots.get(), count.get(), distance.get(), left, mine, right, total
    )
    total_copy = pltpu.make_async_copy(total, total_far, done.at[11])
    total_copy.start()
    left_copy.wait()
    mine_copy.wait()
    total_copy.wait()


def short_kernel(
    own, slots, count, distance, left, mine, total, w_message, out,
    own_in, slots_in, count_in, distance_in, left_in, mine_in, total_in, w_message_in, right, done,
):
    left = Held(left, left_in, done.at[0])
    slots = Held(slots, slots_in, done.at[1])
    count = Held(count, count_in, done.at[2])
    distance = Held(distance, distance_in, done.at[3])
    mine = Held(mine, mine_in, done.at[4])
    total = Held(total, total_in, done.at[5])
    w_message = Held(w_message, w_message_in, done.at[6])
    own = Held(own, own_in, done.at[7])
    run_slots(
        FIRST_QUADS, SLOTS // 4, slots.get(), count.get(), distance.get(), left.get(),
        mine.get(), right, total.get(),
    )
    summed = total_in[...].T * (1.0 / SLOTS)
    out[...] = own.get()[...] + dot3(summed, w_message.get()[...])


def update_kernel(block, base, gain, w_up, w_down, out):
    total = base[...] + block[...].reshape(WIDTH, 128).T
    mean = jnp.mean(total * total, axis=1, keepdims=True)
    normed = total * lax.rsqrt(mean + epsilon) * gain[...]
    hidden = dot3(normed, w_up[...])
    hidden = hidden * jax.nn.sigmoid(hidden)
    out[...] = total + dot3(hidden, w_down[...])


def swap(value, axes):
    return lax.all_to_all(value, axes, 0, 0, tiled=True)


def shape(*dims, dtype=f32):
    return jax.ShapeDtypeStruct(dims, dtype)


def local(
    features, positions, wavevectors, neighbour_slots, neighbour_count, pair_distance,
    w_self, w_neighbour, w_edge, w_message, spec_filter, norm_gain, w_up, w_down,
):
    devices = 1
    for axis in EVERY:
        devices *= lax.axis_size(axis)
    ahead = [(i, i + 1) for i in range(devices - 1)]

    packed = call(
        pack_kernel, [(shape(16, ROWS, 128), VMEM)],
        [(features, HBM), (positions, HBM), (wavevectors, HBM), (spec_filter, HBM)], 8,
        scratch=[
            VMEM((128, WIDTH), f32), VMEM((3, 128), f32), VMEM((3, 512), jnp.int32),
            VMEM((256, WIDTH), f32),
        ],
        copies=4,
    )
    block = swap(packed, TRADE)
    block, ready = lax.optimization_barrier((block, features))
    before = lax.ppermute(ready, EVERY, ahead)
    after = lax.ppermute(ready, EVERY, [(t, s) for s, t in ahead])
    parts, plane = call(
        forward_kernel,
        [(shape(16 * PART, 128), HBM), (shape(512, 2048, dtype=bf16), VMEM)],
        [(block, VMEM)], 16,
        scratch=[VMEM((832, 2048), bf16), VMEM((16 * PART, 128), f32)],
        flops=10**9, copies=1,
    )
    parts = swap(parts.reshape(16, PART, 128), TOTAL)
    weights, third = call(
        weigh_kernel, [(shape(64, 128), HBM), (shape(16, 2048), HBM)], [(block, VMEM)], 8,
        scratch=[
            VMEM((128, KVEC), bf16), VMEM((96, KVEC), bf16), VMEM((64, 128), f32),
            VMEM((16, 2048), f32),
        ],
        flops=10**9, copies=2,
    )
    filtered = call(
        filter_kernel, [(shape(16, PART, 128), HBM)], [(parts, VMEM), (weights, HBM)], 4,
        scratch=[VMEM((64, 128), f32), VMEM((PART, 128), f32)],
        copies=17,
    )
    filtered = swap(filtered, TOTAL)
    lists = [
        (neighbour_slots, HBM), (neighbour_count.reshape(1, 128), HBM), (pair_distance, HBM),
    ]
    lists_in = [VMEM((32, 128), jnp.int32), VMEM((1, 128), jnp.int32), VMEM((32, 128), f32)]
    left, mine, total = call(
        ready_kernel,
        [(shape(WIDTH, 896, dtype=bf16), HBM), (shape(WIDTH, 128), HBM),
         (shape(WIDTH, 128), HBM)],
        [(before, VMEM), (features, HBM), (after, VMEM), (w_self, HBM), (w_neighbour, HBM),
         (w_edge, HBM)] + lists, 16,
        scratch=[
            VMEM((128, WIDTH), f32),
            VMEM((WIDTH, WIDTH), f32), VMEM((WIDTH, WIDTH), f32), VMEM((RADIAL, WIDTH), f32),
        ] + lists_in + [
            VMEM((WIDTH, 896), bf16), VMEM((WIDTH, 128), f32), VMEM((WIDTH, 128), f32),
            VMEM((896, 512), bf16),
        ],
        flops=2 * 10**9, copies=12,
    )
    beads = call(
        inverse_kernel, [(shape(16, FEATS, 128), HBM)],
        [(filtered.reshape(16 * PART, 128), VMEM), (third, HBM), (plane, VMEM)], 8,
        scratch=[
            VMEM((416, 512), bf16), VMEM((16, 2048), f32),
            VMEM((16, FEATS, 128), f32),
        ],
        flops=10**9, copies=9,
    )
    beads = swap(beads, TRADE)
    base = call(
        short_kernel, [(shape(128, WIDTH), VMEM)],
        [(features, HBM)] + lists + [(left, HBM), (mine, HBM), (total, HBM), (w_message, HBM)],
        12,
        scratch=[VMEM((128, WIDTH), f32)] + lists_in + [
            VMEM((WIDTH, 896), bf16), VMEM((WIDTH, 128), f32), VMEM((WIDTH, 128), f32),
            VMEM((WIDTH, WIDTH), f32), VMEM((896, 512), bf16),
        ],
        flops=2 * 896 * 512 * 4096, copies=8,
    )
    return call(
        update_kernel, [(shape(128, WIDTH), VMEM)],
        [(beads, VMEM), (base, VMEM), (norm_gain.reshape(1, WIDTH), VMEM), (w_up, VMEM),
         (w_down, VMEM)], 12,
    )


def solution(mesh):
    fine = Mesh(mesh.devices.reshape(4, 4, 2, 4, 2), EVERY)
    placed = (
        P(EVERY, None),
        P(None, EVERY),
        P(None, ("zh", "zl")),
        P(None, EVERY),
        P(EVERY),
        P(None, EVERY),
        P(),
        P(),
        P(),
        P(),
        P(("zh", "zl"), None),
        P(),
        P(),
        P(),
    )

    return jax.shard_map(
        local, mesh=fine, in_specs=placed, out_specs=P(EVERY, None), check_vma=False
    )
```

```python
import jax
import jax.numpy as jnp
from jax import lax
from jax.experimental import pallas as pl
from jax.experimental.pallas import tpu as pltpu
from jax.sharding import Mesh, PartitionSpec as P


KVEC = 4096
WIDTH = 512
SLOTS = 32
RADIAL = 16
epsilon = 1e-05
reach = 2.5

TRADE = ("core", "zh", "zl")
TOTAL = ("x", "y")
EVERY = ("x", "y", "core", "zh", "zl")
FEATS = 32
AT_POS = 32
AT_VEC = 35
AT_FILTER = 41
ROWS = 48
PART = 56
USED = tuple(range(7)) + tuple(range(9, 15))

SIN = (6.283182792843448, -41.3414193330158, 81.59613740878913, -76.57967400034956,
       41.20368207513971, -12.268761447381701)
COS = (0.9999999890563522, -19.73920449855691, 64.93911741205494, -85.45013861232991,
       60.16762307755092, -25.967568454487537, 6.528613369793176)

bf16 = jnp.bfloat16
f32 = jnp.float32
NT = (((1,), (1,)), ((), ()))


def halves(value):
    high = value.astype(bf16)
    return high, (value - high.astype(f32)).astype(bf16)


def dot(left, right):
    return jnp.dot(left, right, preferred_element_type=f32)


def dot_nt(left, right):
    return lax.dot_general(left, right, NT, preferred_element_type=f32)


def dot3(left, right):
    left_high, left_low = halves(left)
    right_high, right_low = halves(right)
    return dot(left_high, right_high) + (dot(left_high, right_low) + dot(left_low, right_high))


def turn(cycles):
    part = cycles - jnp.round(cycles)
    square = part * part
    cosine = jnp.full_like(square, COS[-1])
    for factor in COS[-2::-1]:
        cosine = cosine * square + factor
    sine = jnp.full_like(square, SIN[-1])
    for factor in SIN[-2::-1]:
        sine = sine * square + factor
    return cosine, sine * part


class Held:
    def __init__(self, source, target, done):
        self.copy = pltpu.make_async_copy(source, target, done)
        self.target = target
        self.waiting = True
        self.copy.start()

    def get(self):
        if self.waiting:
            self.copy.wait()
            self.waiting = False
        return self.target


HBM = pltpu.HBM
VMEM = pltpu.VMEM


def call(kernel, outs, ins, mib, scratch=(), flops=0, copies=0):
    size = sum(v.size * v.dtype.itemsize for v, _ in ins)
    result = pl.pallas_call(
        kernel,
        out_shape=tuple(HBM(v.shape, v.dtype) if space is HBM else v for v, space in outs),
        in_specs=[pl.BlockSpec(memory_space=space) for _, space in ins],
        out_specs=tuple(pl.BlockSpec(memory_space=space) for _, space in outs),
        scratch_shapes=list(scratch) + [pltpu.SemaphoreType.DMA((copies,))] * (copies > 0),
        compiler_params=pltpu.CompilerParams(vmem_limit_bytes=mib * 1024 * 1024),
        cost_estimate=pl.CostEstimate(flops=flops, bytes_accessed=size, transcendentals=0),
    )(*[pltpu.with_memory_space_constraint(v, HBM) if space is HBM else v for v, space in ins])
    return result if len(outs) > 1 else result[0]


def pack_kernel(
    features, positions, vectors, filters, out, features_in, positions_in, vectors_in, filters_in,
    done,
):
    place = lax.axis_index("x") * 4 + lax.axis_index("y")
    first = pl.multiple_of(lax.axis_index("core") * 256, 256)
    filters = Held(filters.at[pl.ds(first, 256)], filters_in, done.at[0])
    features = Held(features, features_in, done.at[1])
    vectors = Held(vectors, vectors_in, done.at[2])
    positions = Held(positions, positions_in, done.at[3])
    chosen = lax.broadcasted_iota(jnp.int32, (32, WIDTH), 1) == (
        lax.broadcasted_iota(jnp.int32, (32, WIDTH), 0) * 16 + place
    )
    chosen = chosen.astype(f32).astype(bf16)
    high, low = halves(filters.get()[...])
    picked = dot_nt(chosen, high) + dot_nt(chosen, low)
    turned = features.get()[...].T
    own = vectors.get()[:, pl.ds(first, 256)].astype(f32)
    positions = positions.get()
    coords = positions[...]
    for peer in range(16):
        out[peer, 0:FEATS, :] = turned[peer * FEATS : peer * FEATS + FEATS, :]
        out[peer, AT_POS : AT_POS + 3, :] = coords
        for half in range(2):
            lanes = slice(half * 128, half * 128 + 128)
            out[peer, AT_VEC + 3 * half : AT_VEC + 3 * half + 3, :] = own[:, lanes]
            out[peer, AT_FILTER + 2 * half : AT_FILTER + 2 * half + 2, :] = picked[
                2 * peer : 2 * peer + 2, lanes
            ]
        out[peer, ROWS - 3 : ROWS, :] = jnp.zeros((3, 128), f32)


def weigh_kernel(block, out_far, third_far, hot, rows, out, third_out, done):
    number = lax.broadcasted_iota(jnp.int32, (8, 128), 0).astype(f32)
    for source in range(16):
        lanes = slice(source * 128, source * 128 + 128)
        cosine, sine = turn(number * block[source, AT_POS + 2 : AT_POS + 3, :])
        third_out[0:8, lanes] = cosine
        third_out[8:16, lanes] = sine
    third_copy = pltpu.make_async_copy(third_out, third_far, done.at[0])
    third_copy.start()
    pair = lax.broadcasted_iota(jnp.int32, (128, 128), 0).astype(f32)
    row = lax.broadcasted_iota(jnp.int32, (32, 128), 0)
    third = (row // 2).astype(f32)
    odd = (row % 2) == 1
    for source in range(16):
        for half in range(2):
            at = AT_VEC + 3 * half
            n1 = block[source, at : at + 1, :]
            n2 = block[source, at + 1 : at + 2, :]
            n3 = block[source, at + 2 : at + 3, :]
            negative = (n1 < 0) | ((n1 == 0) & (n2 < 0))
            sign = jnp.where(negative, -1.0, 1.0)
            n2 = sign * n2
            n3 = sign * n3
            index = 16.0 * (sign * n1) + jnp.where(n2 >= 0, n2, 8.0 - n2)
            index3 = jnp.where(n3 >= 0, n3, 8.0 - n3)
            lanes = slice((2 * source + half) * 128, (2 * source + half) * 128 + 128)
            hot[:, lanes] = (pair == index).astype(f32).astype(bf16)
            at = AT_FILTER + 2 * half
            value = jnp.where(odd, block[source, at + 1 : at + 2, :], block[source, at : at + 1, :])
            match = (third == index3).astype(f32)
            high, low = halves(match * value)
            rows[0:32, lanes] = high
            rows[32:64, lanes] = low
            rows[64:96, lanes] = match.astype(bf16)
    result = dot_nt(rows[...], hot[...])
    out[0:32, :] = result[0:32] + result[32:64]
    out[32:64, :] = result[64:96]
    copy = pltpu.make_async_copy(out, out_far, done.at[1])
    copy.start()
    third_copy.wait()
    copy.wait()


def forward_kernel(block, out_far, plane, left, out, done):
    number = lax.broadcasted_iota(jnp.int32, (8, 128), 0).astype(f32)
    blank = jnp.zeros((16, 2048), bf16)
    for at in range(112, 512, 128):
        plane[at : at + 16, :] = blank

    for source in range(16):
        lanes = slice(source * 128, source * 128 + 128)
        cos1, sin1 = turn(number * block[source, AT_POS : AT_POS + 1, :])
        cos2, sin2 = turn(number * block[source, AT_POS + 1 : AT_POS + 2, :])
        cos3, sin3 = turn(number * block[source, AT_POS + 2 : AT_POS + 3, :])
        for n1 in range(7):
            cosine, sine = cos1[n1 : n1 + 1, :], sin1[n1 : n1 + 1, :]
            cc, ss = cosine * cos2, sine * sin2
            sc, cs = sine * cos2, cosine * sin2
            wave = jnp.concatenate([cc - ss, cc + ss], axis=0)
            high, low = halves(wave)
            at = 16 * n1
            plane[at : at + 16, lanes] = high
            plane[256 + at : 272 + at, lanes] = low
            wave = jnp.concatenate([sc + cs, sc - cs], axis=0)
            high, low = halves(wave)
            at = 128 + 16 * n1
            plane[at : at + 16, lanes] = high
            plane[256 + at : 272 + at, lanes] = low
        feats = block[source, 0:FEATS, :]
        for at, j in enumerate(USED):
            basis = cos3[j : j + 1, :] if j < 8 else sin3[j - 8 : j - 7, :]
            high, low = halves(basis * feats)
            left[32 * at : 32 * at + 32, lanes] = high
            left[416 + 32 * at : 416 + 32 * at + 32, lanes] = low

    wide, tall = [], []
    for chunk in range(8):
        lanes = slice(chunk * 256, chunk * 256 + 256)
        wide += [left[0:416, lanes], left[0:416, lanes], left[416:832, lanes]]
        tall += [plane[0:256, lanes], plane[256:512, lanes], plane[0:256, lanes]]
    result = dot_nt(jnp.concatenate(wide, axis=1), jnp.concatenate(tall, axis=1))
    for half in range(2):
        lanes = slice(128 * half, 128 * half + 128)
        for row in (52, 53):
            out[pl.ds(2 * half + row, 16, stride=PART), :] = jnp.zeros((16, 128), f32)
        for at, j in enumerate(USED):
            for side in range(2):
                start = 32 * at + 16 * side
                rows = pl.ds(26 * half + 2 * at + side, 16, stride=PART)
                out[rows, :] = result[start : start + 16, lanes]
    copy = pltpu.make_async_copy(out, out_far, done.at[0])
    copy.start()
    copy.wait()


def filter_kernel(parts, weights_far, out_far, weights_in, out, done):
    weights = Held(weights_far, weights_in, done.at[16])
    total = parts[0]
    for source in range(1, 16):
        total = total + parts[source]
    weights = weights.get()
    row = lax.broadcasted_iota(jnp.int32, (16, 128), 0)
    cc, sc = total[0:16], total[26:42]
    cs = jnp.where(row < 2, 0.0, total[12:28])
    ss = jnp.where(row < 2, 0.0, total[38:54])
    plus, minus = weights[0:16, :], weights[16:32, :]
    plus_count, minus_count = weights[32:48, :], weights[48:64, :]
    cos_plus, cos_minus = cc - ss, cc + ss
    sin_plus, sin_minus = sc + cs, sc - cs
    energy = plus_count * (cos_plus * cos_plus + sin_plus * sin_plus)
    energy = energy + minus_count * (cos_minus * cos_minus + sin_minus * sin_minus)
    energy = jnp.sum(energy, axis=1, keepdims=True)
    odd = (lax.broadcasted_iota(jnp.int32, (16, 1), 0) % 2) == 1
    power_odd = jnp.sum(jnp.where(odd, energy, 0.0), axis=0, keepdims=True)
    power_even = jnp.sum(jnp.where(odd, 0.0, energy), axis=0, keepdims=True)
    power = jnp.where(odd, power_odd, power_even)
    scale = lax.rsqrt(power / (2 * KVEC) + epsilon) * (1.0 / 64.0)
    plus, minus = plus * scale, minus * scale
    cos_plus, cos_minus = plus * cos_plus, minus * cos_minus
    sin_plus, sin_minus = plus * sin_plus, minus * sin_minus
    out[0:14, :] = (cos_plus + cos_minus)[0:14]
    out[14:26, :] = (sin_plus - sin_minus)[2:14]
    out[26:40, :] = (sin_plus + sin_minus)[0:14]
    out[40:52, :] = (cos_minus - cos_plus)[2:14]
    out[52:56, :] = jnp.zeros((4, 128), f32)
    copies = [
        pltpu.make_async_copy(out, out_far.at[peer], done.at[peer]) for peer in range(16)
    ]
    for copy in copies:
        copy.start()
    for copy in copies:
        copy.wait()


def inverse_kernel(block, third_far, plane, out_far, left, third_in, out, done):
    third = Held(third_far, third_in, done.at[8])
    for at, j in enumerate(USED):
        for side in range(2):
            start = 32 * at + 16 * side
            for half in range(2):
                rows = pl.ds(26 * half + 2 * at + side, 16, stride=PART)
                high, low = halves(block[rows, :])
                lane = 128 * half
                left[start : start + 16, lane : lane + 128] = high
                left[start : start + 16, 256 + lane : 384 + lane] = low

    third = third.get()

    def send(step):
        rows = pl.ds(2 * step, 2)
        return pltpu.make_async_copy(out.at[rows], out_far.at[rows], done.at[step])

    def tile(step, carry):
        lanes = pl.ds(pl.multiple_of(step * 256, 256), 256)
        upper, lower = plane[0:256, lanes], plane[256:512, lanes]
        wide = dot(
            jnp.concatenate([left[:, 0:256], left[:, 0:256], left[:, 256:512]], axis=1),
            jnp.concatenate([upper, lower, upper], axis=0),
        )
        basis = third[:, lanes]
        total = jnp.zeros((FEATS, 256), f32)
        for at, j in enumerate(USED):
            total = total + basis[j : j + 1, :] * wide[32 * at : 32 * at + 32]
        out[2 * step] = total[:, 0:128]
        out[2 * step + 1] = total[:, 128:256]
        send(step).start()
        return carry

    lax.fori_loop(0, 8, tile, 0, unroll=8)
    for step in range(8):
        send(step).wait()


def run_slots(low, high, slots, count, distance, left, mine, right, total):
    right[432:512, :] = jnp.zeros((80, 512), bf16)
    window = lax.broadcasted_iota(jnp.int32, (384, 128), 0)
    spacing = reach / (RADIAL - 1)
    centers = lax.broadcasted_iota(jnp.int32, (RADIAL, 128), 0).astype(f32) * spacing
    live = count[...]

    def step(quad, carry):
        for pair in range(2):
            for side in range(2):
                slot = 4 * quad + 2 * pair + side
                lanes = slice(256 * pair + side * 128, 256 * pair + side * 128 + 128)
                wanted = slots[pl.ds(slot, 1), :]
                hot = (window == wanted).astype(f32).astype(bf16)
                right[0:384, lanes] = hot
                right[512:896, lanes] = hot
                offset = (distance[pl.ds(slot, 1), :] - centers) / spacing
                upper, lower = halves(jnp.exp(-(offset * offset)))
                right[384:400, lanes] = upper
                right[400:416, lanes] = upper
                right[416:432, lanes] = lower
            wide = dot(left[...], right[:, 256 * pair : 256 * pair + 256])
            added = total[...]
            for side in range(2):
                half = wide[:, side * 128 : side * 128 + 128] + mine[...]
                message = half + half * jnp.tanh(half)
                valid = (4 * quad + 2 * pair + side < live).astype(f32)
                added = added + message * valid
            total[...] = added
        return carry

    lax.fori_loop(low, high, step, 0)


FIRST_QUADS = 2


def ready_kernel(
    paired, own, other, w_self, w_neighbour, w_edge, slots, count, distance,
    left_far, mine_far, total_far,
    own_in, w_self_in, w_neighbour_in, w_edge_in, slots_in, count_in,
    distance_in, left, mine, total, right, done,
):
    w_neighbour = Held(w_neighbour, w_neighbour_in, done.at[0])
    own = Held(own, own_in, done.at[1])
    w_self = Held(w_self, w_self_in, done.at[4])
    w_edge = Held(w_edge, w_edge_in, done.at[5])
    slots = Held(slots, slots_in, done.at[6])
    count = Held(count, count_in, done.at[7])
    distance = Held(distance, distance_in, done.at[8])
    nb_high, nb_low = halves(0.5 * w_neighbour.get()[...])
    odd = jnp.full((128, WIDTH), lax.axis_index("zl"), jnp.int32) == 1
    paired, other = paired[...], other[...]
    before, after = jnp.where(odd, paired, other), jnp.where(odd, other, paired)
    for at, part in ((0, before), (256, after), (128, own.get()[...])):
        high, low = halves(part)
        projected = dot(high, nb_high) + (dot(high, nb_low) + dot(low, nb_high))
        high, low = halves(projected.T)
        left[:, at : at + 128] = high
        left[:, 512 + at : 640 + at] = low
    edge_high, edge_low = halves(0.5 * w_edge.get()[...])
    edge_high, edge_low = edge_high.astype(f32), edge_low.astype(f32)
    blank = jnp.zeros((80, WIDTH), f32)
    edges = jnp.concatenate([edge_high, edge_low, edge_high, blank], axis=0)
    left[:, 384:512] = edges.T.astype(bf16)
    left_copy = pltpu.make_async_copy(left, left_far, done.at[9])
    left_copy.start()
    mine[...] = (0.5 * dot3(own_in[...], w_self.get()[...])).T
    mine_copy = pltpu.make_async_copy(mine, mine_far, done.at[10])
    mine_copy.start()
    total[...] = jnp.zeros_like(total)
    run_slots(
        0, FIRST_QUADS, slots.get(), count.get(), distance.get(), left, mine, right, total
    )
    total_copy = pltpu.make_async_copy(total, total_far, done.at[11])
    total_copy.start()
    left_copy.wait()
    mine_copy.wait()
    total_copy.wait()


def short_kernel(
    own, slots, count, distance, left, mine, total, w_message, out,
    own_in, slots_in, count_in, distance_in, left_in, mine_in, total_in, w_message_in, right, done,
):
    left = Held(left, left_in, done.at[0])
    slots = Held(slots, slots_in, done.at[1])
    count = Held(count, count_in, done.at[2])
    distance = Held(distance, distance_in, done.at[3])
    mine = Held(mine, mine_in, done.at[4])
    total = Held(total, total_in, done.at[5])
    w_message = Held(w_message, w_message_in, done.at[6])
    own = Held(own, own_in, done.at[7])
    run_slots(
        FIRST_QUADS, SLOTS // 4, slots.get(), count.get(), distance.get(), left.get(),
        mine.get(), right, total.get(),
    )
    summed = total_in[...].T * (1.0 / SLOTS)
    out[...] = own.get()[...] + dot3(summed, w_message.get()[...])


def update_kernel(block, base, gain, w_up, w_down, out):
    total = base[...] + block[...].reshape(WIDTH, 128).T
    mean = jnp.mean(total * total, axis=1, keepdims=True)
    normed = total * lax.rsqrt(mean + epsilon) * gain[...]
    hidden = dot3(normed, w_up[...])
    hidden = hidden * jax.nn.sigmoid(hidden)
    out[...] = total + dot3(hidden, w_down[...])


def swap(value, axes):
    return lax.all_to_all(value, axes, 0, 0, tiled=True)


def shape(*dims, dtype=f32):
    return jax.ShapeDtypeStruct(dims, dtype)


def local(
    features, positions, wavevectors, neighbour_slots, neighbour_count, pair_distance,
    w_self, w_neighbour, w_edge, w_message, spec_filter, norm_gain, w_up, w_down,
):
    devices = 1
    for axis in EVERY:
        devices *= lax.axis_size(axis)
    inner = [(i, i ^ 1) for i in range(devices)]
    outer = [(i, i + 1) for i in range(1, devices - 1, 2)]
    outer = outer + [(t, s) for s, t in outer]

    packed = call(
        pack_kernel, [(shape(16, ROWS, 128), VMEM)],
        [(features, HBM), (positions, HBM), (wavevectors, HBM), (spec_filter, HBM)], 8,
        scratch=[
            VMEM((128, WIDTH), f32), VMEM((3, 128), f32), VMEM((3, 512), jnp.int32),
            VMEM((256, WIDTH), f32),
        ],
        copies=4,
    )
    block = swap(packed, TRADE)
    block, ready = lax.optimization_barrier((block, features))
    paired = lax.ppermute(ready, EVERY, inner)
    other = lax.ppermute(ready, EVERY, outer)
    parts, plane = call(
        forward_kernel,
        [(shape(16 * PART, 128), HBM), (shape(512, 2048, dtype=bf16), VMEM)],
        [(block, VMEM)], 16,
        scratch=[VMEM((832, 2048), bf16), VMEM((16 * PART, 128), f32)],
        flops=10**9, copies=1,
    )
    parts = swap(parts.reshape(16, PART, 128), TOTAL)
    weights, third = call(
        weigh_kernel, [(shape(64, 128), HBM), (shape(16, 2048), HBM)], [(block, VMEM)], 8,
        scratch=[
            VMEM((128, KVEC), bf16), VMEM((96, KVEC), bf16), VMEM((64, 128), f32),
            VMEM((16, 2048), f32),
        ],
        flops=10**9, copies=2,
    )
    filtered = call(
        filter_kernel, [(shape(16, PART, 128), HBM)], [(parts, VMEM), (weights, HBM)], 4,
        scratch=[VMEM((64, 128), f32), VMEM((PART, 128), f32)],
        copies=17,
    )
    filtered = swap(filtered, TOTAL)
    lists = [
        (neighbour_slots, HBM), (neighbour_count.reshape(1, 128), HBM), (pair_distance, HBM),
    ]
    lists_in = [VMEM((32, 128), jnp.int32), VMEM((1, 128), jnp.int32), VMEM((32, 128), f32)]
    left, mine, total = call(
        ready_kernel,
        [(shape(WIDTH, 896, dtype=bf16), HBM), (shape(WIDTH, 128), HBM),
         (shape(WIDTH, 128), HBM)],
        [(paired, VMEM), (features, HBM), (other, VMEM), (w_self, HBM), (w_neighbour, HBM),
         (w_edge, HBM)] + lists, 16,
        scratch=[
            VMEM((128, WIDTH), f32),
            VMEM((WIDTH, WIDTH), f32), VMEM((WIDTH, WIDTH), f32), VMEM((RADIAL, WIDTH), f32),
        ] + lists_in + [
            VMEM((WIDTH, 896), bf16), VMEM((WIDTH, 128), f32), VMEM((WIDTH, 128), f32),
            VMEM((896, 512), bf16),
        ],
        flops=2 * 10**9, copies=12,
    )
    beads = call(
        inverse_kernel, [(shape(16, FEATS, 128), HBM)],
        [(filtered.reshape(16 * PART, 128), VMEM), (third, HBM), (plane, VMEM)], 8,
        scratch=[
            VMEM((416, 512), bf16), VMEM((16, 2048), f32),
            VMEM((16, FEATS, 128), f32),
        ],
        flops=10**9, copies=9,
    )
    beads = swap(beads, TRADE)
    base = call(
        short_kernel, [(shape(128, WIDTH), VMEM)],
        [(features, HBM)] + lists + [(left, HBM), (mine, HBM), (total, HBM), (w_message, HBM)],
        12,
        scratch=[VMEM((128, WIDTH), f32)] + lists_in + [
            VMEM((WIDTH, 896), bf16), VMEM((WIDTH, 128), f32), VMEM((WIDTH, 128), f32),
            VMEM((WIDTH, WIDTH), f32), VMEM((896, 512), bf16),
        ],
        flops=2 * 896 * 512 * 4096, copies=8,
    )
    return call(
        update_kernel, [(shape(128, WIDTH), VMEM)],
        [(beads, VMEM), (base, VMEM), (norm_gain.reshape(1, WIDTH), VMEM), (w_up, VMEM),
         (w_down, VMEM)], 12,
    )


def solution(mesh):
    fine = Mesh(mesh.devices.reshape(4, 4, 2, 4, 2), EVERY)
    placed = (
        P(EVERY, None),
        P(None, EVERY),
        P(None, ("zh", "zl")),
        P(None, EVERY),
        P(EVERY),
        P(None, EVERY),
        P(),
        P(),
        P(),
        P(),
        P(("zh", "zl"), None),
        P(),
        P(),
        P(),
    )

    return jax.shard_map(
        local, mesh=fine, in_specs=placed, out_specs=P(EVERY, None), check_vma=False
    )
```

```python
import jax
import jax.numpy as jnp
from jax import lax
from jax.experimental import pallas as pl
from jax.experimental.pallas import tpu as pltpu
from jax.sharding import Mesh, PartitionSpec as P


KVEC = 4096
WIDTH = 512
SLOTS = 32
RADIAL = 16
epsilon = 1e-05
reach = 2.5

TRADE = ("core", "zh", "zl")
TOTAL = ("x", "y")
EVERY = ("x", "y", "core", "zh", "zl")
FEATS = 32
AT_POS = 32
AT_VEC = 35
AT_FILTER = 41
ROWS = 48
PART = 56
USED = tuple(range(7)) + tuple(range(9, 15))

SIN = (6.283182792843448, -41.3414193330158, 81.59613740878913, -76.57967400034956,
       41.20368207513971, -12.268761447381701)
COS = (0.9999999890563522, -19.73920449855691, 64.93911741205494, -85.45013861232991,
       60.16762307755092, -25.967568454487537, 6.528613369793176)

bf16 = jnp.bfloat16
f32 = jnp.float32
NT = (((1,), (1,)), ((), ()))


def halves(value):
    high = value.astype(bf16)
    return high, (value - high.astype(f32)).astype(bf16)


def dot(left, right):
    return jnp.dot(left, right, preferred_element_type=f32)


def dot_nt(left, right):
    return lax.dot_general(left, right, NT, preferred_element_type=f32)


def dot3(left, right):
    left_high, left_low = halves(left)
    right_high, right_low = halves(right)
    return dot(left_high, right_high) + (dot(left_high, right_low) + dot(left_low, right_high))


def turn(cycles):
    part = cycles - jnp.round(cycles)
    square = part * part
    cosine = jnp.full_like(square, COS[-1])
    for factor in COS[-2::-1]:
        cosine = cosine * square + factor
    sine = jnp.full_like(square, SIN[-1])
    for factor in SIN[-2::-1]:
        sine = sine * square + factor
    return cosine, sine * part


class Held:
    def __init__(self, source, target, done):
        self.copy = pltpu.make_async_copy(source, target, done)
        self.target = target
        self.waiting = True
        self.copy.start()

    def get(self):
        if self.waiting:
            self.copy.wait()
            self.waiting = False
        return self.target


HBM = pltpu.HBM
VMEM = pltpu.VMEM


def call(kernel, outs, ins, mib, scratch=(), flops=0, copies=0):
    size = sum(v.size * v.dtype.itemsize for v, _ in ins)
    result = pl.pallas_call(
        kernel,
        out_shape=tuple(HBM(v.shape, v.dtype) if space is HBM else v for v, space in outs),
        in_specs=[pl.BlockSpec(memory_space=space) for _, space in ins],
        out_specs=tuple(pl.BlockSpec(memory_space=space) for _, space in outs),
        scratch_shapes=list(scratch) + [pltpu.SemaphoreType.DMA((copies,))] * (copies > 0),
        compiler_params=pltpu.CompilerParams(vmem_limit_bytes=mib * 1024 * 1024),
        cost_estimate=pl.CostEstimate(flops=flops, bytes_accessed=size, transcendentals=0),
    )(*[pltpu.with_memory_space_constraint(v, HBM) if space is HBM else v for v, space in ins])
    return result if len(outs) > 1 else result[0]


def pack_kernel(
    features, positions, vectors, filters, out, features_in, positions_in, vectors_in, filters_in,
    done,
):
    place = lax.axis_index("x") * 4 + lax.axis_index("y")
    first = pl.multiple_of(lax.axis_index("core") * 256, 256)
    features = Held(features, features_in, done.at[1])
    filters = Held(filters.at[pl.ds(first, 256)], filters_in, done.at[0])
    vectors = Held(vectors, vectors_in, done.at[2])
    positions = Held(positions, positions_in, done.at[3])
    turned = features.get()[...].T
    for peer in range(16):
        out[peer, 0:FEATS, :] = turned[peer * FEATS : peer * FEATS + FEATS, :]
    chosen = lax.broadcasted_iota(jnp.int32, (32, WIDTH), 1) == (
        lax.broadcasted_iota(jnp.int32, (32, WIDTH), 0) * 16 + place
    )
    chosen = chosen.astype(f32).astype(bf16)
    own = vectors.get()[:, pl.ds(first, 256)].astype(f32)
    coords = positions.get()[...]
    high, low = halves(filters.get()[...])
    picked = dot_nt(chosen, high) + dot_nt(chosen, low)
    for peer in range(16):
        out[peer, AT_POS : AT_POS + 3, :] = coords
        for half in range(2):
            lanes = slice(half * 128, half * 128 + 128)
            out[peer, AT_VEC + 3 * half : AT_VEC + 3 * half + 3, :] = own[:, lanes]
            out[peer, AT_FILTER + 2 * half : AT_FILTER + 2 * half + 2, :] = picked[
                2 * peer : 2 * peer + 2, lanes
            ]
        out[peer, ROWS - 3 : ROWS, :] = jnp.zeros((3, 128), f32)


def weigh_kernel(block, out_far, third_far, hot, rows, out, third_out, done):
    number = lax.broadcasted_iota(jnp.int32, (8, 128), 0).astype(f32)
    for source in range(16):
        lanes = slice(source * 128, source * 128 + 128)
        cosine, sine = turn(number * block[source, AT_POS + 2 : AT_POS + 3, :])
        third_out[0:8, lanes] = cosine
        third_out[8:16, lanes] = sine
    third_copy = pltpu.make_async_copy(third_out, third_far, done.at[0])
    third_copy.start()
    pair = lax.broadcasted_iota(jnp.int32, (128, 128), 0).astype(f32)
    row = lax.broadcasted_iota(jnp.int32, (32, 128), 0)
    third = (row // 2).astype(f32)
    odd = (row % 2) == 1
    for source in range(16):
        for half in range(2):
            at = AT_VEC + 3 * half
            n1 = block[source, at : at + 1, :]
            n2 = block[source, at + 1 : at + 2, :]
            n3 = block[source, at + 2 : at + 3, :]
            negative = (n1 < 0) | ((n1 == 0) & (n2 < 0))
            sign = jnp.where(negative, -1.0, 1.0)
            n2 = sign * n2
            n3 = sign * n3
            index = 16.0 * (sign * n1) + jnp.where(n2 >= 0, n2, 8.0 - n2)
            index3 = jnp.where(n3 >= 0, n3, 8.0 - n3)
            lanes = slice((2 * source + half) * 128, (2 * source + half) * 128 + 128)
            hot[:, lanes] = (pair == index).astype(f32).astype(bf16)
            at = AT_FILTER + 2 * half
            value = jnp.where(odd, block[source, at + 1 : at + 2, :], block[source, at : at + 1, :])
            match = (third == index3).astype(f32)
            high, low = halves(match * value)
            rows[0:32, lanes] = high
            rows[32:64, lanes] = low
            rows[64:96, lanes] = match.astype(bf16)
    result = dot_nt(rows[...], hot[...])
    out[0:32, :] = result[0:32] + result[32:64]
    out[32:64, :] = result[64:96]
    copy = pltpu.make_async_copy(out, out_far, done.at[1])
    copy.start()
    third_copy.wait()
    copy.wait()


def forward_kernel(block, out_far, plane, left, out, done):
    number = lax.broadcasted_iota(jnp.int32, (8, 128), 0).astype(f32)
    blank = jnp.zeros((16, 2048), bf16)
    for at in range(112, 512, 128):
        plane[at : at + 16, :] = blank

    for source in range(16):
        lanes = slice(source * 128, source * 128 + 128)
        cos1, sin1 = turn(number * block[source, AT_POS : AT_POS + 1, :])
        cos2, sin2 = turn(number * block[source, AT_POS + 1 : AT_POS + 2, :])
        cos3, sin3 = turn(number * block[source, AT_POS + 2 : AT_POS + 3, :])
        for n1 in range(7):
            cosine, sine = cos1[n1 : n1 + 1, :], sin1[n1 : n1 + 1, :]
            cc, ss = cosine * cos2, sine * sin2
            sc, cs = sine * cos2, cosine * sin2
            wave = jnp.concatenate([cc - ss, cc + ss], axis=0)
            high, low = halves(wave)
            at = 16 * n1
            plane[at : at + 16, lanes] = high
            plane[256 + at : 272 + at, lanes] = low
            wave = jnp.concatenate([sc + cs, sc - cs], axis=0)
            high, low = halves(wave)
            at = 128 + 16 * n1
            plane[at : at + 16, lanes] = high
            plane[256 + at : 272 + at, lanes] = low
        feats = block[source, 0:FEATS, :]
        for at, j in enumerate(USED):
            basis = cos3[j : j + 1, :] if j < 8 else sin3[j - 8 : j - 7, :]
            high, low = halves(basis * feats)
            left[32 * at : 32 * at + 32, lanes] = high
            left[416 + 32 * at : 416 + 32 * at + 32, lanes] = low

    wide, tall = [], []
    for chunk in range(8):
        lanes = slice(chunk * 256, chunk * 256 + 256)
        wide += [left[0:416, lanes], left[0:416, lanes], left[416:832, lanes]]
        tall += [plane[0:256, lanes], plane[256:512, lanes], plane[0:256, lanes]]
    result = dot_nt(jnp.concatenate(wide, axis=1), jnp.concatenate(tall, axis=1))
    for half in range(2):
        lanes = slice(128 * half, 128 * half + 128)
        for row in (52, 53):
            out[pl.ds(2 * half + row, 16, stride=PART), :] = jnp.zeros((16, 128), f32)
        for at, j in enumerate(USED):
            for side in range(2):
                start = 32 * at + 16 * side
                rows = pl.ds(26 * half + 2 * at + side, 16, stride=PART)
                out[rows, :] = result[start : start + 16, lanes]
    copy = pltpu.make_async_copy(out, out_far, done.at[0])
    copy.start()
    copy.wait()


def filter_kernel(parts, weights_far, out_far, weights_in, out, done):
    weights = Held(weights_far, weights_in, done.at[16])
    total = parts[0]
    for source in range(1, 16):
        total = total + parts[source]
    weights = weights.get()
    row = lax.broadcasted_iota(jnp.int32, (16, 128), 0)
    cc, sc = total[0:16], total[26:42]
    cs = jnp.where(row < 2, 0.0, total[12:28])
    ss = jnp.where(row < 2, 0.0, total[38:54])
    plus, minus = weights[0:16, :], weights[16:32, :]
    plus_count, minus_count = weights[32:48, :], weights[48:64, :]
    cos_plus, cos_minus = cc - ss, cc + ss
    sin_plus, sin_minus = sc + cs, sc - cs
    energy = plus_count * (cos_plus * cos_plus + sin_plus * sin_plus)
    energy = energy + minus_count * (cos_minus * cos_minus + sin_minus * sin_minus)
    energy = jnp.sum(energy, axis=1, keepdims=True)
    odd = (lax.broadcasted_iota(jnp.int32, (16, 1), 0) % 2) == 1
    power_odd = jnp.sum(jnp.where(odd, energy, 0.0), axis=0, keepdims=True)
    power_even = jnp.sum(jnp.where(odd, 0.0, energy), axis=0, keepdims=True)
    power = jnp.where(odd, power_odd, power_even)
    scale = lax.rsqrt(power / (2 * KVEC) + epsilon) * (1.0 / 64.0)
    plus, minus = plus * scale, minus * scale
    cos_plus, cos_minus = plus * cos_plus, minus * cos_minus
    sin_plus, sin_minus = plus * sin_plus, minus * sin_minus
    out[0:14, :] = (cos_plus + cos_minus)[0:14]
    out[14:26, :] = (sin_plus - sin_minus)[2:14]
    out[26:40, :] = (sin_plus + sin_minus)[0:14]
    out[40:52, :] = (cos_minus - cos_plus)[2:14]
    out[52:56, :] = jnp.zeros((4, 128), f32)
    copies = [
        pltpu.make_async_copy(out, out_far.at[peer], done.at[peer]) for peer in range(16)
    ]
    for copy in copies:
        copy.start()
    for copy in copies:
        copy.wait()


def inverse_kernel(block, third_far, plane, out_far, left, third_in, out, done):
    third = Held(third_far, third_in, done.at[8])
    for at, j in enumerate(USED):
        for side in range(2):
            start = 32 * at + 16 * side
            for half in range(2):
                rows = pl.ds(26 * half + 2 * at + side, 16, stride=PART)
                high, low = halves(block[rows, :])
                lane = 128 * half
                left[start : start + 16, lane : lane + 128] = high
                left[start : start + 16, 256 + lane : 384 + lane] = low

    third = third.get()

    def send(step):
        rows = pl.ds(2 * step, 2)
        return pltpu.make_async_copy(out.at[rows], out_far.at[rows], done.at[step])

    def tile(step, carry):
        lanes = pl.ds(pl.multiple_of(step * 256, 256), 256)
        upper, lower = plane[0:256, lanes], plane[256:512, lanes]
        wide = dot(
            jnp.concatenate([left[:, 0:256], left[:, 0:256], left[:, 256:512]], axis=1),
            jnp.concatenate([upper, lower, upper], axis=0),
        )
        basis = third[:, lanes]
        total = jnp.zeros((FEATS, 256), f32)
        for at, j in enumerate(USED):
            total = total + basis[j : j + 1, :] * wide[32 * at : 32 * at + 32]
        out[2 * step] = total[:, 0:128]
        out[2 * step + 1] = total[:, 128:256]
        send(step).start()
        return carry

    lax.fori_loop(0, 8, tile, 0, unroll=8)
    for step in range(8):
        send(step).wait()


def run_slots(low, high, slots, count, distance, left, mine, right, total):
    right[432:512, :] = jnp.zeros((80, 512), bf16)
    window = lax.broadcasted_iota(jnp.int32, (384, 128), 0)
    spacing = reach / (RADIAL - 1)
    centers = lax.broadcasted_iota(jnp.int32, (RADIAL, 128), 0).astype(f32) * spacing
    live = count[...]

    def step(quad, carry):
        for pair in range(2):
            for side in range(2):
                slot = 4 * quad + 2 * pair + side
                lanes = slice(256 * pair + side * 128, 256 * pair + side * 128 + 128)
                wanted = slots[pl.ds(slot, 1), :]
                hot = (window == wanted).astype(f32).astype(bf16)
                right[0:384, lanes] = hot
                right[512:896, lanes] = hot
                offset = (distance[pl.ds(slot, 1), :] - centers) / spacing
                upper, lower = halves(jnp.exp(-(offset * offset)))
                right[384:400, lanes] = upper
                right[400:416, lanes] = upper
                right[416:432, lanes] = lower
            wide = dot(left[...], right[:, 256 * pair : 256 * pair + 256])
            added = total[...]
            for side in range(2):
                half = wide[:, side * 128 : side * 128 + 128] + mine[...]
                message = half + half * jnp.tanh(half)
                valid = (4 * quad + 2 * pair + side < live).astype(f32)
                added = added + message * valid
            total[...] = added
        return carry

    lax.fori_loop(low, high, step, 0)


FIRST_QUADS = 2


def ready_kernel(
    paired, own, other, w_self, w_neighbour, w_edge, slots, count, distance,
    left_far, mine_far, total_far,
    own_in, w_self_in, w_neighbour_in, w_edge_in, slots_in, count_in,
    distance_in, left, mine, total, right, done,
):
    w_neighbour = Held(w_neighbour, w_neighbour_in, done.at[0])
    own = Held(own, own_in, done.at[1])
    w_self = Held(w_self, w_self_in, done.at[4])
    w_edge = Held(w_edge, w_edge_in, done.at[5])
    slots = Held(slots, slots_in, done.at[6])
    count = Held(count, count_in, done.at[7])
    distance = Held(distance, distance_in, done.at[8])
    nb_high, nb_low = halves(0.5 * w_neighbour.get()[...])
    odd = jnp.full((128, WIDTH), lax.axis_index("zl"), jnp.int32) == 1
    paired, other = paired[...], other[...]
    before, after = jnp.where(odd, paired, other), jnp.where(odd, other, paired)
    for at, part in ((0, before), (256, after), (128, own.get()[...])):
        high, low = halves(part)
        projected = dot(high, nb_high) + (dot(high, nb_low) + dot(low, nb_high))
        high, low = halves(projected.T)
        left[:, at : at + 128] = high
        left[:, 512 + at : 640 + at] = low
    edge_high, edge_low = halves(0.5 * w_edge.get()[...])
    edge_high, edge_low = edge_high.astype(f32), edge_low.astype(f32)
    blank = jnp.zeros((80, WIDTH), f32)
    edges = jnp.concatenate([edge_high, edge_low, edge_high, blank], axis=0)
    left[:, 384:512] = edges.T.astype(bf16)
    left_copy = pltpu.make_async_copy(left, left_far, done.at[9])
    left_copy.start()
    mine[...] = (0.5 * dot3(own_in[...], w_self.get()[...])).T
    mine_copy = pltpu.make_async_copy(mine, mine_far, done.at[10])
    mine_copy.start()
    total[...] = jnp.zeros_like(total)
    run_slots(
        0, FIRST_QUADS, slots.get(), count.get(), distance.get(), left, mine, right, total
    )
    total_copy = pltpu.make_async_copy(total, total_far, done.at[11])
    total_copy.start()
    left_copy.wait()
    mine_copy.wait()
    total_copy.wait()


def short_kernel(
    own, slots, count, distance, left, mine, total, w_message, w_up, w_down, out, w_split,
    own_in, slots_in, count_in, distance_in, left_in, mine_in, total_in, w_message_in, w_up_in,
    w_down_in, right, done,
):
    left = Held(left, left_in, done.at[0])
    slots = Held(slots, slots_in, done.at[1])
    count = Held(count, count_in, done.at[2])
    distance = Held(distance, distance_in, done.at[3])
    mine = Held(mine, mine_in, done.at[4])
    total = Held(total, total_in, done.at[5])
    w_message = Held(w_message, w_message_in, done.at[6])
    own = Held(own, own_in, done.at[7])
    w_up = Held(w_up, w_up_in, done.at[8])
    w_down = Held(w_down, w_down_in, done.at[9])
    run_slots(
        FIRST_QUADS, SLOTS // 4, slots.get(), count.get(), distance.get(), left.get(),
        mine.get(), right, total.get(),
    )
    summed = total_in[...].T * (1.0 / SLOTS)
    out[...] = own.get()[...] + dot3(summed, w_message.get()[...])
    w_split[0], w_split[1] = halves(w_up.get()[...])
    w_split[2], w_split[3] = halves(w_down.get()[...])


def split_dot(left, high, low):
    left_high, left_low = halves(left)
    return dot(left_high, high) + (dot(left_high, low) + dot(left_low, high))


def update_kernel(block, base, gain, weights, out):
    total = base[...] + block[...].reshape(WIDTH, 128).T
    mean = jnp.mean(total * total, axis=1, keepdims=True)
    normed = total * lax.rsqrt(mean + epsilon) * gain[...]
    hidden = split_dot(normed, weights[0], weights[1])
    hidden = hidden * jax.nn.sigmoid(hidden)
    out[...] = total + split_dot(hidden, weights[2], weights[3])


def swap(value, axes):
    return lax.all_to_all(value, axes, 0, 0, tiled=True)


def shape(*dims, dtype=f32):
    return jax.ShapeDtypeStruct(dims, dtype)


def local(
    features, positions, wavevectors, neighbour_slots, neighbour_count, pair_distance,
    w_self, w_neighbour, w_edge, w_message, spec_filter, norm_gain, w_up, w_down,
):
    devices = 1
    for axis in EVERY:
        devices *= lax.axis_size(axis)
    inner = [(i, i ^ 1) for i in range(devices)]
    outer = [(i, i + 1) for i in range(1, devices - 1, 2)]
    outer = outer + [(t, s) for s, t in outer]

    packed = call(
        pack_kernel, [(shape(16, ROWS, 128), VMEM)],
        [(features, HBM), (positions, HBM), (wavevectors, HBM), (spec_filter, HBM)], 8,
        scratch=[
            VMEM((128, WIDTH), f32), VMEM((3, 128), f32), VMEM((3, 512), jnp.int32),
            VMEM((256, WIDTH), f32),
        ],
        copies=4,
    )
    block = swap(packed, TRADE)
    block, ready = lax.optimization_barrier((block, features))
    paired = lax.ppermute(ready, EVERY, inner)
    other = lax.ppermute(ready, EVERY, outer)
    parts, plane = call(
        forward_kernel,
        [(shape(16 * PART, 128), HBM), (shape(512, 2048, dtype=bf16), VMEM)],
        [(block, VMEM)], 16,
        scratch=[VMEM((832, 2048), bf16), VMEM((16 * PART, 128), f32)],
        flops=10**9, copies=1,
    )
    parts = swap(parts.reshape(16, PART, 128), TOTAL)
    weights, third = call(
        weigh_kernel, [(shape(64, 128), HBM), (shape(16, 2048), HBM)], [(block, VMEM)], 8,
        scratch=[
            VMEM((128, KVEC), bf16), VMEM((96, KVEC), bf16), VMEM((64, 128), f32),
            VMEM((16, 2048), f32),
        ],
        flops=10**9, copies=2,
    )
    filtered = call(
        filter_kernel, [(shape(16, PART, 128), HBM)], [(parts, VMEM), (weights, HBM)], 4,
        scratch=[VMEM((64, 128), f32), VMEM((PART, 128), f32)],
        copies=17,
    )
    filtered = swap(filtered, TOTAL)
    lists = [
        (neighbour_slots, HBM), (neighbour_count.reshape(1, 128), HBM), (pair_distance, HBM),
    ]
    lists_in = [VMEM((32, 128), jnp.int32), VMEM((1, 128), jnp.int32), VMEM((32, 128), f32)]
    left, mine, total = call(
        ready_kernel,
        [(shape(WIDTH, 896, dtype=bf16), HBM), (shape(WIDTH, 128), HBM),
         (shape(WIDTH, 128), HBM)],
        [(paired, VMEM), (features, HBM), (other, VMEM), (w_self, HBM), (w_neighbour, HBM),
         (w_edge, HBM)] + lists, 16,
        scratch=[
            VMEM((128, WIDTH), f32),
            VMEM((WIDTH, WIDTH), f32), VMEM((WIDTH, WIDTH), f32), VMEM((RADIAL, WIDTH), f32),
        ] + lists_in + [
            VMEM((WIDTH, 896), bf16), VMEM((WIDTH, 128), f32), VMEM((WIDTH, 128), f32),
            VMEM((896, 512), bf16),
        ],
        flops=2 * 10**9, copies=12,
    )
    beads = call(
        inverse_kernel, [(shape(16, FEATS, 128), HBM)],
        [(filtered.reshape(16 * PART, 128), VMEM), (third, HBM), (plane, VMEM)], 8,
        scratch=[
            VMEM((416, 512), bf16), VMEM((16, 2048), f32),
            VMEM((16, FEATS, 128), f32),
        ],
        flops=10**9, copies=9,
    )
    beads = swap(beads, TRADE)
    base, weights = call(
        short_kernel, [(shape(128, WIDTH), VMEM), (shape(4, WIDTH, WIDTH, dtype=bf16), VMEM)],
        [(features, HBM)] + lists + [(left, HBM), (mine, HBM), (total, HBM), (w_message, HBM),
                                     (w_up, HBM), (w_down, HBM)],
        16,
        scratch=[VMEM((128, WIDTH), f32)] + lists_in + [
            VMEM((WIDTH, 896), bf16), VMEM((WIDTH, 128), f32), VMEM((WIDTH, 128), f32),
            VMEM((WIDTH, WIDTH), f32), VMEM((WIDTH, WIDTH), f32), VMEM((WIDTH, WIDTH), f32),
            VMEM((896, 512), bf16),
        ],
        flops=2 * 896 * 512 * 4096, copies=10,
    )
    return call(
        update_kernel, [(shape(128, WIDTH), VMEM)],
        [(beads, VMEM), (base, VMEM), (norm_gain.reshape(1, WIDTH), VMEM), (weights, VMEM)],
        8,
    )


def solution(mesh):
    fine = Mesh(mesh.devices.reshape(4, 4, 2, 4, 2), EVERY)
    placed = (
        P(EVERY, None),
        P(None, EVERY),
        P(None, ("zh", "zl")),
        P(None, EVERY),
        P(EVERY),
        P(None, EVERY),
        P(),
        P(),
        P(),
        P(),
        P(("zh", "zl"), None),
        P(),
        P(),
        P(),
    )

    return jax.shard_map(
        local, mesh=fine, in_specs=placed, out_specs=P(EVERY, None), check_vma=False
    )
```
